256 devices in a mesh: ctx: 32 (over x_lo, z, core), exp: 8 (over x_hi, y).
Axes of the slice: x: 4 (x_hi: 2, x_lo: 2; x = x_hi * 2 + x_lo), y: 4, z: 8, core: 2. Of those that a mesh axis runs over, the one named last changes fastest.
Arguments:
- queries: bfloat16 [8192, 8192], P('ctx', 'exp'), may hold values from -8 to 8
- keys: bfloat16 [8192, 512], P('ctx'), may hold values from -4 to 4
- values: bfloat16 [8192, 512], P('ctx'), may hold values from -6 to 6
- w_out: bfloat16 [8192, 4096], P('exp'), may hold values from -0.5 to 0.5
- residual: bfloat16 [8192, 4096], P(('ctx', 'exp')), may hold values from -1.5 to 1.5
- norm_gain: bfloat16 [4096], replicated, may hold values from 0.099609375 to 1.8984375
- expert_ids: int32 [8192, 2], P(('ctx', 'exp')), may hold values from 0 to 7, all different within a row; in each aligned block of 32 rows (0 to 31, 32 to 63, ...) at most 16 rows name the same one
- gate_weights: float32 [8192, 2], P(('ctx', 'exp')), may hold values from 0.2 to 1
- w_gate: bfloat16 [8, 4096, 768], P('exp', 'ctx'), may hold values from -0.09375 to 0.09375
- w_up: bfloat16 [8, 4096, 768], P('exp', 'ctx'), may hold values from -0.09375 to 0.09375
- w_down: bfloat16 [8, 768, 4096], P('exp', None, 'ctx'), may hold values from -0.21875 to 0.21875
Outputs:
- layer_out: bfloat16 [8192, 4096], P(('ctx', 'exp'))
The draws below stay inside these ranges and needn't reach their ends.
Inputs may be any that keep to these rules, and one draw needn't show every extreme that they name: `expert_ids`: each row names 2 different experts; within each aligned block of 32 rows (the rows of one device) no expert is named by more than 16 rows.
All inputs are finite; a program needn't handle non-finite values.
Results may differ from the reference program's by a relative error of at most 0.025.
Values may be sent and summed in bfloat16 or wider, within the bound.
A program may use at most 128 MiB of HBM per device.

```python
import math
import jax
import jax.numpy as jnp
import numpy as np
from jax import lax

D = 4096
HQ = 64
KVH = 4
HD = 128
FF = 768
TOPK = 2
SEQ = 8192
EXPERTS = 8
ROWS = 32
CAP = 16


def draw_keys(key, part):
    shape = (SEQ, KVH * HD)
    base = jnp.clip(jax.random.normal(jax.random.fold_in(key, 1), shape, jnp.float32), -4.0, 4.0)
    return base.astype(jnp.bfloat16)


def draw_queries(key, part):
    shape = (SEQ, HQ * HD)
    base = jnp.clip(jax.random.normal(jax.random.fold_in(key, 2), shape, jnp.float32), -6.0, 6.0)
    return base.astype(jnp.bfloat16)


def levels(stream_key, shape, cuts, smallest, high):
    level, own = 1.0, jax.random.fold_in(stream_key, 6)
    for position, shards_of in cuts:
        steps = jnp.exp(jax.random.uniform(jax.random.fold_in(own, position), (shards_of,), jnp.float32, smallest / len(cuts), high / len(cuts)))
        level = level * jnp.repeat(steps, shape[position] // shards_of).reshape([-1 if axis == position else 1 for axis in range(len(shape))])
    return level


def deal_out(rng, own, number, rows, count, top, reach, slope):
    sequence = jax.random.permutation(rng, count)
    heavy_load, common = load_shares(count, rows * top, reach, slope, True), load_shares(count, rows * top, reach, slope, False)
    places = jnp.arange(count)

    def named(sizes, turn):
        used = int((sizes > 0).sum())
        fixed = max(1, used // 4)
        shifted = fixed + (places - fixed + turn * (used - fixed)) % max(1, count - fixed)
        return jnp.zeros((count,), jnp.int32).at[sequence[jnp.where(places < fixed, places, shifted)]].set(jnp.asarray(sizes, jnp.int32))

    sizes = jnp.where(number % 4 == 0, named(heavy_load, number // 4), named(common, number - number // 4 - 1))
    mixed = jax.random.permutation(jax.random.fold_in(own, 3), count)
    donor, sink = mixed[0:count // 2 * 2:2], mixed[1:count // 2 * 2:2]
    slack = jnp.minimum(sizes[donor] - 1, reach - sizes[sink]) // 2
    slack = jnp.where((donor == sequence[0]) | (sink == sequence[0]) | (sizes[sink] == 0), 0, jnp.maximum(slack, 0))
    shifted = jax.random.randint(jax.random.fold_in(own, 4), (count // 2,), 0, 1 << 20) % (slack + 1)
    sizes = sizes.at[donor].add(-shifted).at[sink].add(shifted)
    members = jnp.searchsorted(jnp.cumsum(sizes), jnp.arange(rows * top), side="right").astype(jnp.int32)
    grid = members.reshape(top, rows).T
    grid = grid[jax.random.permutation(jax.random.fold_in(own, 1), rows)]
    turn = jax.random.randint(jax.random.fold_in(own, 2), (rows, 1), 0, top)
    return jnp.take_along_axis(grid, (jnp.arange(top)[None, :] + turn) % top, axis=1)


def load_shares(count, total, most, lean, full):
    portions = [(1 << 20) // math.isqrt(grade ** lean) + 1 for grade in range(1, count + 1)]
    largest = most if full else min(most, max(-(-total // count), total * portions[0] // sum(portions)))
    least = 1 if total - largest >= count - 1 else 0
    given, rest = [largest] + [least] * (count - 1), total - largest - least * (count - 1)
    while rest > 0:
        movable = [i for i in range(1, count) if given[i] < largest] or [i for i in range(1, count) if given[i] < most]
        whole, left = sum([portions[i] for i in movable]), rest
        for i in movable:
            more = min(most - given[i], max(1, left * portions[i] // whole), rest)
            given[i] = given[i] + more
            rest = rest - more
    return np.array(given)


def normal_values(stream_key, shape, spread, reach, split=(), kind=jnp.bfloat16):
    loudness = levels(stream_key, shape, split, -0.22, 0.18) if split else 1.0
    result = jax.random.normal(stream_key, shape, jnp.float32) * spread * loudness
    return jnp.minimum(jnp.maximum(result, -reach), reach).astype(kind)


def setup_inputs(seed: int = 0) -> dict:
    seeds = jax.random.split(jax.random.key(seed), 12)
    queries = draw_queries(jax.random.fold_in(seeds[11], 71), 0)
    keys = draw_keys(jax.random.fold_in(seeds[11], 71), 0)
    values = normal_values(seeds[2], (SEQ, KVH * HD), 1.0, 6.0, ((0, 32),))
    w_out = normal_values(seeds[3], (HQ * HD, D), HD ** -0.5, 0.5, ((0, 8),))
    residual = normal_values(seeds[4], (SEQ, D), 0.25, 1.5, ((0, 256),))
    norm_gain = jnp.clip(1.0 + 0.18 * jax.random.normal(seeds[5], (D,), jnp.float32), 0.099609375, 1.8984375).astype(jnp.bfloat16)
    expert_ids_keys = jax.random.split(jax.random.fold_in(seeds[6], 1), SEQ // ROWS)
    expert_ids_turns = jax.random.permutation(jax.random.fold_in(seeds[6], 3), SEQ // ROWS)
    expert_ids = jax.vmap(lambda own, number: deal_out(jax.random.fold_in(seeds[6], 2), own, number, ROWS, EXPERTS, TOPK, CAP, 2))(expert_ids_keys, expert_ids_turns).reshape((SEQ, TOPK))
    gate_weights = jnp.clip(0.2 + 0.8 * jax.random.uniform(seeds[7], (SEQ, TOPK), jnp.float32) ** levels(seeds[7], (SEQ, TOPK), ((0, 256),), -0.2, 0.2), 0.2, 1.0)
    w_gate = normal_values(seeds[8], (EXPERTS, D, FF), D ** -0.5, 0.09375, ((0, 8), (1, 32)))
    w_up = normal_values(seeds[9], (EXPERTS, D, FF), D ** -0.5, 0.09375, ((0, 8), (1, 32)))
    w_down = normal_values(seeds[10], (EXPERTS, FF, D), FF ** -0.5, 0.21875, ((0, 8), (2, 32)))
    return {"queries": queries, "keys": keys, "values": values, "w_out": w_out, "residual": residual, "norm_gain": norm_gain, "expert_ids": expert_ids, "gate_weights": gate_weights, "w_gate": w_gate, "w_up": w_up, "w_down": w_down}


def attention_all(queries, keys, values):
    group = HQ // KVH
    qblk = 512 if SEQ % 512 == 0 else SEQ
    blocks_per_head = SEQ // qblk
    scale = 1.0 / math.sqrt(HD)
    key_pos = jnp.arange(SEQ, dtype=jnp.int32)

    def one_block(index):
        head = index // blocks_per_head
        block = index % blocks_per_head
        kv_head = head // group
        rows = lax.dynamic_slice(queries, (block * qblk, head * HD), (qblk, HD))
        key_cols = lax.dynamic_slice_in_dim(keys, kv_head * HD, HD, 1)
        value_cols = lax.dynamic_slice_in_dim(values, kv_head * HD, HD, 1)
        scores = jnp.dot(rows, key_cols.T, preferred_element_type=jnp.float32) * scale
        query_pos = block * qblk + jnp.arange(qblk, dtype=jnp.int32)
        allowed = key_pos[None, :] <= query_pos[:, None]
        scores = jnp.where(allowed, scores, -jnp.inf)
        top = lax.optimization_barrier(jnp.max(scores, axis=1, keepdims=True))
        probs = jnp.exp(scores - top)
        total = lax.optimization_barrier(jnp.sum(probs, axis=1))
        mixed = jnp.dot(probs.astype(jnp.bfloat16), value_cols, preferred_element_type=jnp.float32)
        return (mixed / total[:, None]).astype(jnp.bfloat16)
    blocks = lax.map(one_block, jnp.arange(HQ * blocks_per_head, dtype=jnp.int32))
    return blocks.reshape(HQ, SEQ, HD).transpose(1, 0, 2).reshape(SEQ, HQ * HD)

def reference(queries, keys, values, w_out, residual, norm_gain, expert_ids, gate_weights, w_gate, w_up, w_down):
    attn = attention_all(queries, keys, values)
    projected = jnp.dot(attn, w_out, preferred_element_type=jnp.float32)
    hidden_state = (residual.astype(jnp.float32) + projected).astype(jnp.bfloat16)
    state_f = hidden_state.astype(jnp.float32)
    inv_rms = 1.0 / jnp.sqrt(lax.optimization_barrier(jnp.mean(state_f * state_f, axis=1, keepdims=True)) + 1e-06)
    normed = (state_f * inv_rms * norm_gain.astype(jnp.float32)[None, :]).astype(jnp.bfloat16)
    flat_ids = expert_ids.reshape(-1)
    flat_gates = gate_weights.reshape(-1)
    most_rows = SEQ // ROWS * CAP

    def expert_step(acc, expert):
        hit = flat_ids == expert
        count = jnp.sum(hit.astype(jnp.int32))
        pairs = jnp.nonzero(hit, size=most_rows, fill_value=0)[0].astype(jnp.int32)
        valid = jnp.arange(most_rows, dtype=jnp.int32) < count
        token = pairs // TOPK
        rows = normed[token]
        gate_pre = jnp.dot(rows, w_gate[expert], preferred_element_type=jnp.float32)
        up_pre = jnp.dot(rows, w_up[expert], preferred_element_type=jnp.float32)
        expert_hidden = (jax.nn.silu(gate_pre) * up_pre).astype(jnp.bfloat16)
        expert_result = jnp.dot(expert_hidden, w_down[expert], preferred_element_type=jnp.float32).astype(jnp.bfloat16)
        weight = jnp.where(valid, flat_gates[pairs], jnp.zeros_like(flat_gates[pairs]))
        acc = acc.at[token].add(weight[:, None] * expert_result.astype(jnp.float32))
        return (acc, None)
    acc, _ = lax.scan(expert_step, jnp.zeros((SEQ, D), jnp.float32), jnp.arange(EXPERTS, dtype=jnp.int32))
    return (state_f + acc).astype(jnp.bfloat16)
```

```python
import functools
import math

import jax
import jax.numpy as jnp
from jax import lax
from jax.experimental import pallas as pl
from jax.experimental.pallas import tpu as pltpu
from jax.sharding import PartitionSpec as P

D = 4096
HQ = 64
KVH = 4
HD = 128
FF = 768
EXPERTS = 8
CAP = 16
ROWS = 32
NX, NZ, NC = 2, 8, 2
CTX = NX * NZ * NC
EXP = 8
TOK = 256
HALF = 128
HEADS = HQ // EXP
MESH = pl.DeviceIdType.MESH
MIB = 1 << 20
F32 = jnp.float32
BF16 = jnp.bfloat16


def remote(src, dst, send, recv, ctx, exp):
    return pltpu.make_async_remote_copy(
        src_ref=src, dst_ref=dst, send_sem=send, recv_sem=recv, device_id=(ctx, exp), device_id_type=MESH
    )


def greet(peers):
    barrier = pltpu.get_barrier_semaphore()
    for ctx, exp in peers:
        pl.semaphore_signal(barrier, inc=1, device_id=(ctx, exp), device_id_type=MESH)
    pl.semaphore_wait(barrier, len(peers))


def place():
    me = lax.axis_index("ctx")
    return me, lax.axis_index("exp"), me // (NZ * NC), (me // NC) % NZ, me % NC


def chunk(x, z, core):
    return x * (NZ * NC) + lax.rem(z + 2 * NZ, NZ) * NC + core


def chip(x, z):
    return x * NZ + lax.rem(z + 2 * NZ, NZ)


def hop_copies(w_ref, hop, snd, rcv, slot):
    me, ex, x, z, core = place()
    out = []
    for way, (xx, step) in enumerate(((x, 1), (1 - x, -1))):
        ref = w_ref.at[chip(xx, z - step * hop)]
        out.append(remote(ref, ref, snd.at[slot, way], rcv.at[slot, way], chunk(x, z + step, core), ex))
    return out


def start_hop(*a):
    for c in hop_copies(*a):
        c.start()


def finish_hop(w_ref, hop, snd, rcv, slot):
    me, ex, x, z, core = place()
    for way, (xx, step) in enumerate(((x, 1), (1 - x, -1))):
        ref = w_ref.at[chip(xx, z - step * (hop + 1))]
        remote(ref, ref, snd.at[slot, way], rcv.at[slot, way], me, ex).wait_recv()
    for c in hop_copies(w_ref, hop, snd, rcv, slot):
        c.wait_send()


def ring_peers():
    me, ex, x, z, core = place()
    return [(chunk(x, z + 1, core), ex), (chunk(x, z - 1, core), ex)]


HBM = pltpu.HBM
TILES = FF // NC // 128
FH = FF // NC
CHIPS = CTX // NC
WSHAPE = jax.ShapeDtypeStruct((CHIPS, NC, 3 * FH, 128), BF16)
ATTN_HOPS, PROJ_HOPS = 1, 4
EXPERT_HOPS = NZ - 1 - ATTN_HOPS - PROJ_HOPS


def gather_kernel(
    k_ref, v_ref, q_ref, g_ref, u_ref, d_ref, kv_ref, qm_ref, w_ref,
    local, ring_s, ring_r, sib_s, sib_r, own_s, own_r, w_l, w_s, w_r, wx_s, wx_r,
):
    me, ex, x, z, core = place()

    up, down = chunk(x, z + 1, core), chunk(x, z - 1, core)
    across, sib, mirror = chunk(1 - x, z, core), chunk(x, z, 1 - core), CTX - 1 - me
    head = pl.ds(pl.multiple_of((ex // 2) * HD, HD), HD)
    copies = [
        pltpu.make_async_copy(k_ref.at[:, head], kv_ref.at[me, 0], local.at[0]),
        pltpu.make_async_copy(v_ref.at[:, head], kv_ref.at[me, 1], local.at[1]),
    ]
    here = chip(x, z)

    def pieces(half):
        for a, ref in enumerate((g_ref, u_ref)):
            for t in range(TILES):
                cols = pl.ds(pl.multiple_of(half * FH + t * 128, 128), 128)
                yield ref.at[:, cols], w_ref.at[here, core, pl.ds((a * TILES + t) * 128, 128)]
        yield d_ref.at[pl.ds(pl.multiple_of(half * FH, FH), FH)], w_ref.at[here, core, pl.ds(2 * FH, FH)]

    kept = [pltpu.make_async_copy(src, dst, w_l.at[i]) for i, (src, dst) in enumerate(pieces(core))]
    for c in copies + kept:
        c.start()
    greet([(up, ex), (down, ex), (across, ex), (sib, ex), (mirror, ex)])
    for c in copies:
        c.wait()
    sent = []

    def send(*a):
        c = remote(*a, ex)
        c.start()
        sent.append(c)
        return c

    xs = (x, 1 - x)

    def piece(stream, step):
        which, kv = stream // 2, stream % 2
        zz = z - step if kv == 0 else z + step
        return kv_ref.at[chunk(xs[which], zz, core), kv]

    def hop(stream, step):
        ref = piece(stream, step)
        return send(ref, ref, ring_s.at[stream, step], ring_r.at[stream, step], up if stream % 2 == 0 else down)

    def landed(stream, step):
        ref = piece(stream, step + 1)
        remote(ref, ref, ring_s.at[stream, step], ring_r.at[stream, step], me, ex).wait_recv()

    own = kv_ref.at[me]
    for stream in (0, 1):
        hop(stream, 0)
    a = send(own, own, own_s.at[0], own_r.at[0], across)
    send(own, own, own_s.at[1], own_r.at[1], sib)
    for i, (src, dst) in enumerate(pieces(1 - core)):
        send(src, dst, w_s.at[i], w_r.at[i], sib)
    send(q_ref.at[pl.ds(HALF, HALF)], qm_ref, own_s.at[2], own_r.at[2], mirror)
    other = kv_ref.at[across]
    remote(other, other, own_s.at[0], own_r.at[0], me, ex).wait_recv()
    for stream in (2, 3):
        hop(stream, 0)
    send(other, other, own_s.at[3], own_r.at[3], sib)
    for i, (src, dst) in enumerate(pieces(core)):
        kept[i].wait()
        remote(src, dst, w_s.at[i], w_r.at[i], me, ex).wait_recv()
    send(w_ref.at[here], w_ref.at[here], wx_s, wx_r, across)
    for step in range(NZ - 1):
        for stream in range(4):
            landed(stream, step)
            if step + 1 < NZ - 1:
                hop(stream, step + 1)
            ref = piece(stream, step + 1)
            send(ref, ref, sib_s.at[stream, step], sib_r.at[stream, step], sib)
    for stream in range(4):
        which, kv = stream // 2, stream % 2
        for step in range(NZ - 1):
            zz = z - step - 1 if kv == 0 else z + step + 1
            ref = kv_ref.at[chunk(xs[which], zz, 1 - core), kv]
            remote(ref, ref, sib_s.at[stream, step], sib_r.at[stream, step], me, ex).wait_recv()
    ref = kv_ref.at[sib]
    remote(ref, ref, own_s.at[1], own_r.at[1], me, ex).wait_recv()
    ref = kv_ref.at[chunk(1 - x, z, 1 - core)]
    remote(ref, ref, own_s.at[3], own_r.at[3], me, ex).wait_recv()
    beside = w_ref.at[chip(1 - x, z)]
    remote(beside, beside, wx_s, wx_r, me, ex).wait_recv()
    remote(qm_ref, qm_ref, own_s.at[2], own_r.at[2], me, ex).wait_recv()
    for c in sent:
        c.wait_send()


def gather(keys, values, queries, w_gate, w_up, w_down):
    n = 2 * TILES + 1
    return pl.pallas_call(
        gather_kernel,
        out_shape=(
            jax.ShapeDtypeStruct((CTX, 2, TOK, HD), BF16),
            jax.ShapeDtypeStruct((HALF, HEADS * HD), BF16),
            WSHAPE,
        ),
        in_specs=[pl.BlockSpec(memory_space=pl.ANY)] * 6,
        out_specs=(
            pl.BlockSpec(memory_space=pltpu.VMEM),
            pl.BlockSpec(memory_space=pltpu.VMEM),
            pl.BlockSpec(memory_space=HBM),
        ),
        scratch_shapes=[
            pltpu.SemaphoreType.DMA((2,)),
            pltpu.SemaphoreType.DMA((4, NZ - 1)),
            pltpu.SemaphoreType.DMA((4, NZ - 1)),
            pltpu.SemaphoreType.DMA((4, NZ - 1)),
            pltpu.SemaphoreType.DMA((4, NZ - 1)),
            pltpu.SemaphoreType.DMA((4,)),
            pltpu.SemaphoreType.DMA((4,)),
            pltpu.SemaphoreType.DMA((n,)),
            pltpu.SemaphoreType.DMA((n,)),
            pltpu.SemaphoreType.DMA((n,)),
            pltpu.SemaphoreType.DMA,
            pltpu.SemaphoreType.DMA,
        ],
        compiler_params=pltpu.CompilerParams(collective_id=1, has_side_effects=True, vmem_limit_bytes=16 * MIB),
        cost_estimate=pl.CostEstimate(flops=0, bytes_accessed=64 * MIB, transcendentals=0),
        name="kv_gather",
    )(keys, values, queries, w_gate, w_up, w_down)


KB = 1024
CHUNKS = KB // TOK
TR = 128
QROWS = HEADS * HALF
SCALE2 = math.log2(math.e) / math.sqrt(HD)


def attn_kernel(q_ref, qm_ref, kv_ref, w_in, oa_ref, om_ref, w_ref, qs, acc, m_sc, vx, snd, rcv):
    greet(ring_peers())
    start_hop(w_ref, 0, snd, rcv, 0)
    me = lax.axis_index("ctx")
    starts = (me * TOK, (CTX - 1 - me) * TOK + HALF)
    vx[:, HD:] = jnp.ones((KB, HD), BF16)
    for which, (src, dst) in enumerate(((q_ref, oa_ref), (qm_ref, om_ref))):
        start = starts[which]
        for h in range(HEADS):
            qs[pl.ds(h * HALF, HALF), :] = src[:, pl.ds(h * HD, HD)]
        m_sc[...] = jnp.full_like(m_sc, -1e30)
        acc[...] = jnp.zeros_like(acc)

        def block(j, masked, start=start):
            k = kv_ref[pl.ds(CHUNKS * j, CHUNKS), 0].reshape(KB, HD)
            vx[:, :HD] = kv_ref[pl.ds(CHUNKS * j, CHUNKS), 1].reshape(KB, HD)
            for t in range(QROWS // TR):
                rows = pl.ds(t * TR, TR)
                s = lax.dot_general(qs[rows, :], k, (((1,), (1,)), ((), ())), preferred_element_type=F32)
                if masked:
                    row = lax.broadcasted_iota(jnp.int32, (TR, KB), 0) % HALF + start
                    col = lax.broadcasted_iota(jnp.int32, (TR, KB), 1) + j * KB
                    s = jnp.where(col <= row, s, -1e30)
                old = m_sc[rows, :]
                new = jnp.maximum(old, jnp.max(s, axis=1, keepdims=True))
                p = jnp.exp2((s - new[:, :1]) * SCALE2)
                factor = jnp.exp2((old - new) * SCALE2)
                m_sc[rows, :] = new
                acc[rows, :] = acc[rows, :] * jnp.concatenate([factor, factor], axis=1) + jnp.dot(
                    p.astype(BF16), vx[...], preferred_element_type=F32
                )

        full = start // KB
        lax.fori_loop(0, full, lambda j, c: (block(j, False), c)[1], 0)
        block(full, True)
        for h in range(HEADS):
            rows = pl.ds(h * HALF, HALF)
            dst[:, pl.ds(h * HD, HD)] = (acc[rows, :HD] / acc[rows, HD:]).astype(BF16)
    finish_hop(w_ref, 0, snd, rcv, 0)


def attention(queries, mirrored, kv, weights):
    half = jax.ShapeDtypeStruct((HALF, HEADS * HD), BF16)
    vmem, hbm = pl.BlockSpec(memory_space=pltpu.VMEM), pl.BlockSpec(memory_space=HBM)
    return pl.pallas_call(
        attn_kernel,
        out_shape=(half, half, WSHAPE),
        in_specs=[vmem, vmem, vmem, hbm],
        out_specs=(vmem, vmem, hbm),
        input_output_aliases={3: 2},
        scratch_shapes=[
            pltpu.VMEM((QROWS, HD), BF16),
            pltpu.VMEM((QROWS, 2 * HD), F32),
            pltpu.VMEM((QROWS, HD), F32),
            pltpu.VMEM((KB, 2 * HD), BF16),
            pltpu.SemaphoreType.DMA((ATTN_HOPS, 2)),
            pltpu.SemaphoreType.DMA((ATTN_HOPS, 2)),
        ],
        compiler_params=pltpu.CompilerParams(collective_id=4, has_side_effects=True, vmem_limit_bytes=32 * MIB),
        cost_estimate=pl.CostEstimate(flops=9_000_000_000, bytes_accessed=6 * MIB, transcendentals=9_000_000),
        name="attention",
    )(queries, mirrored, kv, weights)


def slots(ids_ref):
    lane = lax.broadcasted_iota(jnp.int32, (ROWS, EXPERTS * CAP), 1)
    named = [ids_ref[:, k : k + 1] == lane // CAP for k in range(2)]
    has = (named[0] | named[1]).astype(F32)
    tri = lax.broadcasted_iota(jnp.int32, (ROWS, ROWS), 1) < lax.broadcasted_iota(jnp.int32, (ROWS, ROWS), 0)
    place = jnp.dot(tri.astype(F32).astype(BF16), has.astype(BF16), preferred_element_type=F32)
    here = place == (lane % CAP).astype(F32)
    return [(n & here).astype(F32) for n in named]


NB = 512


def project_kernel(
    oa_ref, om_ref, w_hbm, res_ref, gain_ref, ids_ref, e_in, arr_ref, hid_ref, e_ref,
    w, back, part, recv, norm, out, w_sem, back_s, back_r, rs_s, rs_r, a_s, a_r, f_s, f_r, snd, rcv,
):
    me, ex = lax.axis_index("ctx"), lax.axis_index("exp")
    mirror, sib = CTX - 1 - me, me + 1 - 2 * (me % NC)
    load = pltpu.make_async_copy(w_hbm, w, w_sem)
    load.start()
    peers = [lax.rem(ex + d, EXP) for d in range(1, EXP)]
    greet(ring_peers() + [(mirror, ex), (sib, ex)] + [(me, p) for p in peers])
    give = remote(om_ref, back, back_s, back_r, mirror, ex)
    give.start()
    start_hop(e_ref, ATTN_HOPS, snd, rcv, 0)
    load.wait()

    def next_hop(i):
        finish_hop(e_ref, ATTN_HOPS + i, snd, rcv, i)
        if i + 1 < PROJ_HOPS:
            start_hop(e_ref, ATTN_HOPS + i + 1, snd, rcv, i + 1)

    def half(src, first):
        @pl.loop(0, D // NB)
        def _(n):
            cols = pl.ds(pl.multiple_of(n * NB, NB), NB)
            got = jnp.dot(src[...], w[:, cols], preferred_element_type=F32).astype(BF16)
            for b in range(4):
                part[first + b, :, cols] = got[b * ROWS : (b + 1) * ROWS, :]

    def share(d):
        p = lax.rem(ex + d, EXP)
        return p, remote(part.at[p], recv.at[d - 1], rs_s.at[d - 1], rs_r.at[d - 1], me, p)

    def share_half(first):
        for d in range(1, EXP):
            p, copy = share(d)

            @pl.when((p >= first) & (p < first + 4))
            def _():
                copy.start()

    half(oa_ref, 0)
    share_half(0)
    give.wait_recv()
    half(back, 4)
    share_half(4)
    next_hop(0)
    next_hop(1)
    for d in range(1, EXP):
        share(d)[1].wait_recv()

    @pl.loop(0, D // NB)
    def _(n):
        cols = pl.ds(pl.multiple_of(n * NB, NB), NB)
        total = part[ex, :, cols].astype(F32)
        for d in range(EXP - 1):
            total += recv[d, :, cols].astype(F32)
        hid_ref[:, cols] = (res_ref[:, cols].astype(F32) + total).astype(BF16)

    state = hid_ref[...].astype(F32)
    inv = 1.0 / jnp.sqrt(jnp.mean(state * state, axis=1, keepdims=True) + 1e-06)
    norm[...] = (state * inv * gain_ref[...].astype(F32)).astype(BF16)
    first, second = slots(ids_ref)
    table = (first + second).T.astype(BF16)
    out[...] = jnp.dot(table, norm[...], preferred_element_type=F32).astype(BF16).reshape(EXPERTS, CAP, D)

    def give_rows(d):
        p = lax.rem(ex + d, EXP)
        return remote(out.at[p], arr_ref.at[0, ex], a_s.at[d - 1], a_r.at[d - 1], me, p)

    def forward(d):
        source = lax.rem(ex + EXP - d, EXP)
        return remote(arr_ref.at[0, source], arr_ref.at[1, source], f_s.at[d], f_r.at[d], sib, ex)

    for d in range(1, EXP):
        give_rows(d).start()
    arr_ref[0, ex] = out[ex]
    forward(0).start()
    next_hop(2)
    for d in range(1, EXP):
        source = lax.rem(ex + EXP - d, EXP)
        remote(out.at[ex], arr_ref.at[0, source], a_s.at[d - 1], a_r.at[d - 1], me, ex).wait_recv()
        forward(d).start()
    for d in range(EXP):
        forward(d).wait()
    next_hop(3)
    give.wait_send()
    for d in range(1, EXP):
        share(d)[1].wait_send()
        give_rows(d).wait_send()


def project(attn_own, attn_mirror, w_out, residual, gain, ids, weights):
    vmem, any_ = pl.BlockSpec(memory_space=pltpu.VMEM), pl.BlockSpec(memory_space=pl.ANY)
    return pl.pallas_call(
        project_kernel,
        out_shape=(
            jax.ShapeDtypeStruct((NC, EXPERTS, CAP, D), BF16),
            jax.ShapeDtypeStruct((ROWS, D), BF16),
            WSHAPE,
        ),
        in_specs=[vmem, vmem, any_, vmem, vmem, vmem, pl.BlockSpec(memory_space=HBM)],
        out_specs=(vmem, vmem, pl.BlockSpec(memory_space=HBM)),
        input_output_aliases={6: 2},
        scratch_shapes=[
            pltpu.VMEM((HEADS * HD, D), BF16),
            pltpu.VMEM((HALF, HEADS * HD), BF16),
            pltpu.VMEM((EXP, ROWS, D), BF16),
            pltpu.VMEM((EXP - 1, ROWS, D), BF16),
            pltpu.VMEM((ROWS, D), BF16),
            pltpu.VMEM((EXPERTS, CAP, D), BF16),
            pltpu.SemaphoreType.DMA,
            pltpu.SemaphoreType.DMA,
            pltpu.SemaphoreType.DMA,
            pltpu.SemaphoreType.DMA((EXP - 1,)),
            pltpu.SemaphoreType.DMA((EXP - 1,)),
            pltpu.SemaphoreType.DMA((EXP - 1,)),
            pltpu.SemaphoreType.DMA((EXP - 1,)),
            pltpu.SemaphoreType.DMA((EXP,)),
            pltpu.SemaphoreType.DMA((EXP,)),
            pltpu.SemaphoreType.DMA((PROJ_HOPS, 2)),
            pltpu.SemaphoreType.DMA((PROJ_HOPS, 2)),
        ],
        compiler_params=pltpu.CompilerParams(collective_id=2, has_side_effects=True, vmem_limit_bytes=40 * MIB),
        cost_estimate=pl.CostEstimate(flops=2_200_000_000, bytes_accessed=64 * MIB, transcendentals=0),
        name="project_dispatch",
    )(attn_own, attn_mirror, w_out, residual, gain, ids, weights)


SLOTS = EXPERTS * CAP
DEPTH = NC * 128
GROUPS = 4
GCOLS = D // GROUPS


def expert_kernel(
    arr_ref, w_in, hid_ref, ids_ref, gates_ref, o_ref, w_hbm,
    w, pre, act, mine, theirs, other, res, got, w_sem, x_s, x_r, r_s, r_r, snd, rcv,
):
    me, ex, x, z, core = place()
    sib = me + 1 - 2 * core
    held = ATTN_HOPS + PROJ_HOPS + 1

    def load(step, way):
        c = chip(x, z - step) if way == 0 else chip(1 - x, z + step)
        return c, pltpu.make_async_copy(w_hbm.at[c], w.at[c], w_sem.at[step, way])

    for step in range(held):
        for way in range(2):
            load(step, way)[1].start()
    peers = [lax.rem(ex + d, EXP) for d in range(1, EXP)]
    greet(ring_peers() + [(sib, ex)] + [(me, p) for p in peers])
    start_hop(w_hbm, held - 1, snd, rcv, 0)
    pre[...] = jnp.zeros_like(pre)

    def use(step):
        for way in range(2):
            j, copy = load(step, way)
            copy.wait()
            cols = pl.ds(pl.multiple_of(j * DEPTH, DEPTH), DEPTH)
            rows = arr_ref[:, :, :, cols].reshape(NC * SLOTS, DEPTH)
            tiles = [
                jnp.concatenate([w[j, c, pl.ds(t * 128, 128)] for c in range(NC)], axis=0) for t in range(2 * TILES)
            ]
            pre[...] += jnp.dot(rows, jnp.concatenate(tiles, axis=1), preferred_element_type=F32)

    @pl.loop(0, held)
    def _(step):
        use(step)

    for i in range(EXPERT_HOPS):
        finish_hop(w_hbm, held - 1 + i, snd, rcv, i)
        if i + 1 < EXPERT_HOPS:
            start_hop(w_hbm, held + i, snd, rcv, i + 1)
        for way in range(2):
            load(held + i, way)[1].start()
        use(held + i)

    gate = pre[:, :FH]
    act[...] = (gate / (1.0 + jnp.exp(-gate)) * pre[:, FH:]).astype(BF16)
    per = CHIPS // GROUPS

    def swap(g):
        return remote(theirs.at[g], other.at[g], x_s.at[g], x_r.at[g], sib, ex)

    def give(g, d):
        p = lax.rem(ex + d, EXP)
        return remote(res.at[g, p], got.at[g, ex], r_s.at[g, d - 1], r_r.at[g, d - 1], me, p)

    def finish(g):
        swap(g).wait_recv()
        res[g] = (mine[g] + other[g]).astype(BF16).reshape(EXPERTS, CAP, GCOLS)
        for d in range(1, EXP):
            give(g, d).start()
        got[g, ex] = res[g, ex]

    for g in range(GROUPS):

        @pl.loop(0, per)
        def _(j):
            down = jnp.concatenate([w[g * per + j, c, pl.ds(2 * FH, FH)] for c in range(NC)], axis=1)
            made = jnp.dot(act[...], down, preferred_element_type=F32)
            cols = pl.ds(pl.multiple_of(j * DEPTH, DEPTH), DEPTH)
            mine[g, :, cols] = made[:SLOTS]
            theirs[g, :, cols] = made[SLOTS:]

        swap(g).start()
        if g >= 1:
            finish(g - 1)
    finish(GROUPS - 1)

    first, second = slots(ids_ref)
    picks = jnp.concatenate([first, second], axis=0).astype(BF16)
    weight = [gates_ref[:, k : k + 1] for k in range(2)]
    for g in range(GROUPS):
        for d in range(1, EXP):
            source = lax.rem(ex + EXP - d, EXP)
            remote(res.at[g, ex], got.at[g, source], r_s.at[g, d - 1], r_r.at[g, d - 1], me, ex).wait_recv()
        both = jnp.dot(picks, got[g].reshape(SLOTS, GCOLS), preferred_element_type=F32)
        total = weight[0] * both[:ROWS] + weight[1] * both[ROWS:]
        cols = pl.ds(g * GCOLS, GCOLS)
        o_ref[:, cols] = (hid_ref[:, cols].astype(F32) + total).astype(BF16)
    for g in range(GROUPS):
        swap(g).wait_send()
        for d in range(1, EXP):
            give(g, d).wait_send()


def experts(arrived, weights, hidden, ids, gates):
    vmem, hbm = pl.BlockSpec(memory_space=pltpu.VMEM), pl.BlockSpec(memory_space=HBM)
    return pl.pallas_call(
        expert_kernel,
        out_shape=(jax.ShapeDtypeStruct((ROWS, D), BF16), WSHAPE),
        in_specs=[vmem, hbm, vmem, vmem, vmem],
        out_specs=(vmem, hbm),
        input_output_aliases={1: 1},
        scratch_shapes=[
            pltpu.VMEM((CHIPS, NC, 3 * FH, 128), BF16),
            pltpu.VMEM((NC * SLOTS, 2 * FH), F32),
            pltpu.VMEM((NC * SLOTS, FH), BF16),
            pltpu.VMEM((GROUPS, SLOTS, GCOLS), F32),
            pltpu.VMEM((GROUPS, SLOTS, GCOLS), F32),
            pltpu.VMEM((GROUPS, SLOTS, GCOLS), F32),
            pltpu.VMEM((GROUPS, EXPERTS, CAP, GCOLS), BF16),
            pltpu.VMEM((GROUPS, EXPERTS, CAP, GCOLS), BF16),
            pltpu.SemaphoreType.DMA((NZ, 2)),
            pltpu.SemaphoreType.DMA((GROUPS,)),
            pltpu.SemaphoreType.DMA((GROUPS,)),
            pltpu.SemaphoreType.DMA((GROUPS, EXP - 1)),
            pltpu.SemaphoreType.DMA((GROUPS, EXP - 1)),
            pltpu.SemaphoreType.DMA((EXPERT_HOPS, 2)),
            pltpu.SemaphoreType.DMA((EXPERT_HOPS, 2)),
        ],
        compiler_params=pltpu.CompilerParams(collective_id=3, has_side_effects=True, vmem_limit_bytes=48 * MIB),
        cost_estimate=pl.CostEstimate(flops=2_500_000_000, bytes_accessed=32 * MIB, transcendentals=100_000),
        name="experts",
    )(arrived, weights, hidden, ids, gates)[0]


def body(queries, keys, values, w_out, residual, norm_gain, expert_ids, gate_weights, w_gate, w_up, w_down):
    kv, mirrored, weights = gather(keys, values, queries, w_gate[0], w_up[0], w_down[0])
    attn_own, attn_mirror, weights = attention(queries[:HALF], mirrored, kv, weights)
    arrived, hidden, weights = project(
        attn_own, attn_mirror, w_out, residual, norm_gain.reshape(1, D), expert_ids, weights
    )
    return experts(arrived, weights, hidden, expert_ids, gate_weights)


def solution(mesh):
    placed = (
        P("ctx", "exp"),
        P("ctx", None),
        P("ctx", None),
        P("exp", None),
        P(("ctx", "exp"), None),
        P(),
        P(("ctx", "exp"), None),
        P(("ctx", "exp"), None),
        P("exp", "ctx", None),
        P("exp", "ctx", None),
        P("exp", None, "ctx"),
    )
    return jax.shard_map(
        body, mesh=mesh, in_specs=placed, out_specs=P(("ctx", "exp"), None), check_vma=False
    )
```

```python
import functools
import math

import jax
import jax.numpy as jnp
from jax import lax
from jax.experimental import pallas as pl
from jax.experimental.pallas import tpu as pltpu
from jax.sharding import PartitionSpec as P

D = 4096
HQ = 64
KVH = 4
HD = 128
FF = 768
EXPERTS = 8
CAP = 16
ROWS = 32
NX, NZ, NC = 2, 8, 2
CTX = NX * NZ * NC
EXP = 8
TOK = 256
HALF = 128
HEADS = HQ // EXP
MESH = pl.DeviceIdType.MESH
MIB = 1 << 20
F32 = jnp.float32
BF16 = jnp.bfloat16


def remote(src, dst, send, recv, ctx, exp):
    return pltpu.make_async_remote_copy(
        src_ref=src, dst_ref=dst, send_sem=send, recv_sem=recv, device_id=(ctx, exp), device_id_type=MESH
    )


def greet(peers):
    barrier = pltpu.get_barrier_semaphore()
    for ctx, exp in peers:
        pl.semaphore_signal(barrier, inc=1, device_id=(ctx, exp), device_id_type=MESH)
    pl.semaphore_wait(barrier, len(peers))


def place():
    me = lax.axis_index("ctx")
    return me, lax.axis_index("exp"), me // (NZ * NC), (me // NC) % NZ, me % NC


def chunk(x, z, core):
    return x * (NZ * NC) + lax.rem(z + 2 * NZ, NZ) * NC + core


def chip(x, z):
    return x * NZ + lax.rem(z + 2 * NZ, NZ)


def hop_copies(w_ref, kind, hop, snd, rcv, slot):
    me, ex, x, z, core = place()
    out = []
    for way, (xx, step) in enumerate(((x, 1), (1 - x, -1))):
        ref = w_ref.at[chip(xx, z - step * hop), :, kind]
        out.append(remote(ref, ref, snd.at[slot, way], rcv.at[slot, way], chunk(x, z + step, core), ex))
    return out


def start_hop(*a):
    for c in hop_copies(*a):
        c.start()


def finish_hop(w_ref, kind, hop, snd, rcv, slot):
    me, ex, x, z, core = place()
    for way, (xx, step) in enumerate(((x, 1), (1 - x, -1))):
        ref = w_ref.at[chip(xx, z - step * (hop + 1)), :, kind]
        remote(ref, ref, snd.at[slot, way], rcv.at[slot, way], me, ex).wait_recv()
    for c in hop_copies(w_ref, kind, hop, snd, rcv, slot):
        c.wait_send()


def ring_peers():
    me, ex, x, z, core = place()
    return [(chunk(x, z + 1, core), ex), (chunk(x, z - 1, core), ex)]


HBM = pltpu.HBM
TILES = FF // NC // 128
FH = FF // NC
CHIPS = CTX // NC
WSHAPE = HBM((CHIPS, NC, 3 * FH, 128), BF16)


def in_hbm(x):
    return pltpu.with_memory_space_constraint(x, HBM)


PRE, DOWN = pl.ds(0, 2 * FH), pl.ds(2 * FH, FH)
ATTN_HOPS, PROJ_HOPS = 1, 5
ATTN_DOWN, PROJ_DOWN = 1, 2
EXPERT_HOPS = NZ - 1 - ATTN_HOPS - PROJ_HOPS
DOWN_HELD = ATTN_DOWN + PROJ_DOWN + 1


CK = NC * TOK
KB = 2 * CK
TR = 128
QROWS = HEADS * HALF
SCALE2 = math.log2(math.e) / math.sqrt(HD)
NP = 2 * TILES + 1


def attn_kernel(
    q_ref, k_ref, v_ref, g_ref, u_ref, d_ref, o_ref, w_ref,
    kv, qs, acc, m_sc, vx,
    kv_l, q_l, own_s, own_r, ring_s, ring_r, sib_s, sib_r, w_l, w_s, w_r, wx_s, wx_r, snd, rcv, d_s, d_r,
):
    me, ex, x, z, core = place()
    up, down = chunk(x, z + 1, core), chunk(x, z - 1, core)
    across, sib = chunk(1 - x, z, core), chunk(x, z, 1 - core)
    here = chip(x, z)
    head = pl.ds(pl.multiple_of((ex // 2) * HD, HD), HD)

    def part(c, cc):
        return kv.at[c, :, pl.ds(pl.multiple_of(cc * TOK, TOK), TOK)]

    def pieces(half):
        for a, ref in enumerate((g_ref, u_ref)):
            for t in range(TILES):
                cols = pl.ds(pl.multiple_of(half * FH + t * 128, 128), 128)
                yield ref.at[:, cols], w_ref.at[here, core, pl.ds((a * TILES + t) * 128, 128)]
        yield d_ref.at[pl.ds(pl.multiple_of(half * FH, FH), FH)], w_ref.at[here, core, pl.ds(2 * FH, FH)]

    rows0 = pl.ds(pl.multiple_of(core * TOK, TOK), TOK)
    kvl = [
        pltpu.make_async_copy(ref.at[:, head], kv.at[here, i, rows0], kv_l.at[i]) for i, ref in enumerate((k_ref, v_ref))
    ]
    ql = [
        pltpu.make_async_copy(
            q_ref.at[pl.ds(a * HALF, HALF), pl.ds(h * HD, HD)], qs.at[a, pl.ds(h * HALF, HALF)], q_l.at[a, h]
        )
        for a in range(2)
        for h in range(HEADS)
    ]
    kept = [pltpu.make_async_copy(src, dst, w_l.at[i]) for i, (src, dst) in enumerate(pieces(core))]
    for c in kvl + ql + kept:
        c.start()
    greet([(up, ex), (down, ex), (across, ex), (sib, ex)])
    for c in kvl:
        c.wait()

    def piece(way, step, cc):
        return part(chip(x, z - step) if way == 0 else chip(1 - x, z + step), cc)

    def hop(way, step):
        ref = piece(way, step, core)
        return remote(ref, ref, ring_s.at[way, step], ring_r.at[way, step], up if way == 0 else down, ex)

    def share(way, step):
        ref = piece(way, step, core)
        return remote(ref, ref, sib_s.at[way, step], sib_r.at[way, step], sib, ex)

    def shared(way, step):
        ref = piece(way, step, 1 - core)
        remote(ref, ref, sib_s.at[way, step], sib_r.at[way, step], me, ex).wait_recv()

    own = part(here, core)
    cross = remote(own, own, own_s, own_r, across, ex)
    cross.start()
    hop(0, 0).start()
    share(0, 0).start()
    other = part(chip(1 - x, z), core)
    remote(other, other, own_s, own_r, me, ex).wait_recv()
    hop(1, 0).start()
    share(1, 0).start()
    wsent = [remote(src, dst, w_s.at[i], w_r.at[i], sib, ex) for i, (src, dst) in enumerate(pieces(1 - core))]
    for c in wsent:
        c.start()
    wcross = remote(w_ref.at[here], w_ref.at[here], wx_s, wx_r, across, ex)
    vx[:, HD:] = jnp.ones((KB, HD), BF16)
    m_sc[...] = jnp.full_like(m_sc, -1e30)
    acc[...] = jnp.zeros_like(acc)
    for c in ql:
        c.wait()

    def block(which, start, c0, c1, masked):
        k = jnp.concatenate([kv[c0, 0], kv[c1, 0]], axis=0)
        for t in range(QROWS // TR):
            rows = pl.ds(t * TR, TR)
            s = lax.dot_general(qs[which, rows, :], k, (((1,), (1,)), ((), ())), preferred_element_type=F32)
            if masked:
                row = lax.broadcasted_iota(jnp.int32, (TR, KB), 0) % HALF + start
                lane = lax.broadcasted_iota(jnp.int32, (TR, KB), 1)
                col = lane + jnp.where(lane < CK, c0 * CK, c1 * CK - CK)
                s = jnp.where(col <= row, s, -1e30)
            old = m_sc[which, rows, :]
            new = jnp.maximum(old, jnp.max(s, axis=1, keepdims=True))
            p = jnp.exp2((s - new[:, :1]) * SCALE2)
            factor = jnp.exp2((old - new) * SCALE2)
            m_sc[which, rows, :] = new
            acc[which, rows, :] = acc[which, rows, :] * jnp.concatenate([factor, factor], axis=1) + jnp.dot(
                p.astype(BF16), vx[...], preferred_element_type=F32
            )

    @pl.loop(0, NZ + 1)
    def _(u):
        step = u + 1

        @pl.when(step < NZ)
        def _():
            for way in range(2):
                ref = piece(way, step, core)
                remote(ref, ref, ring_s.at[way, step - 1], ring_r.at[way, step - 1], me, ex).wait_recv()

                @pl.when(step < NZ - 1)
                def _():
                    hop(way, step).start()

                share(way, step).start()

        @pl.when(u == 2)
        def _():
            for i in range(NP):
                kept[i].wait()
                wsent[i].wait_recv()
            wcross.start()

        @pl.when(u == NZ - 2)
        def _():
            wcross.wait_recv()
            start_hop(w_ref, PRE, 0, snd, rcv, 0)
            start_hop(w_ref, DOWN, 0, d_s, d_r, 0)

        turn = u - 1
        way = lax.rem(turn + 2, 2)
        pair = turn - way

        @pl.when(turn >= 0)
        def _():
            mine = way == 0
            for w in range(2):

                @pl.when(way == w)
                def _():
                    shared(w, pair)
                    shared(w, pair + 1)

            c0 = jnp.where(mine, chip(x, z - pair), chip(1 - x, z + pair))
            c1 = jnp.where(mine, chip(x, z - pair - 1), chip(1 - x, z + pair + 1))
            vx[pl.ds(0, CK), :HD] = kv[c0, 1]
            vx[pl.ds(CK, CK), :HD] = kv[c1, 1]

            @pl.loop(0, 2)
            def _(which):
                start = me * TOK + which * HALF
                full = jnp.maximum(c0, c1) * CK + CK - 1 <= start
                some = jnp.minimum(c0, c1) * CK <= start

                @pl.when(full)
                def _():
                    block(which, start, c0, c1, False)

                @pl.when(some & jnp.logical_not(full))
                def _():
                    block(which, start, c0, c1, True)

    for which in range(2):
        for h in range(HEADS):
            rows = pl.ds(h * HALF, HALF)
            made = (acc[which, rows, :HD] / acc[which, rows, HD:]).astype(BF16)
            o_ref[pl.ds(which * HALF, HALF), pl.ds(h * HD, HD)] = made
    finish_hop(w_ref, PRE, 0, snd, rcv, 0)
    finish_hop(w_ref, DOWN, 0, d_s, d_r, 0)
    cross.wait_send()
    wcross.wait_send()
    for c in wsent:
        c.wait_send()
    for way in range(2):
        for step in range(NZ):
            share(way, step).wait_send()
            if step < NZ - 1:
                hop(way, step).wait_send()


def attention(queries, keys, values, w_gate, w_up, w_down):
    dma = pltpu.SemaphoreType.DMA
    hbm = pl.BlockSpec(memory_space=HBM)
    return pl.pallas_call(
        attn_kernel,
        out_shape=(jax.ShapeDtypeStruct((TOK, HEADS * HD), BF16), WSHAPE),
        in_specs=[hbm] * 6,
        out_specs=(pl.BlockSpec(memory_space=pltpu.VMEM), hbm),
        scratch_shapes=[
            pltpu.VMEM((CHIPS, 2, CK, HD), BF16),
            pltpu.VMEM((2, QROWS, HD), BF16),
            pltpu.VMEM((2, QROWS, 2 * HD), F32),
            pltpu.VMEM((2, QROWS, HD), F32),
            pltpu.VMEM((KB, 2 * HD), BF16),
            dma((2,)), dma((2, HEADS)),
            dma, dma,
            dma((2, NZ - 1)), dma((2, NZ - 1)), dma((2, NZ)), dma((2, NZ)),
            dma((NP,)), dma((NP,)), dma((NP,)), dma, dma,
            dma((ATTN_HOPS, 2)), dma((ATTN_HOPS, 2)), dma((ATTN_DOWN, 2)), dma((ATTN_DOWN, 2)),
        ],
        compiler_params=pltpu.CompilerParams(collective_id=1, has_side_effects=True, vmem_limit_bytes=32 * MIB),
        cost_estimate=pl.CostEstimate(flops=9_000_000_000, bytes_accessed=64 * MIB, transcendentals=9_000_000),
        name="attention",
    )(*(in_hbm(a) for a in (queries, keys, values, w_gate, w_up, w_down)))


def slots(ids_ref):
    lane = lax.broadcasted_iota(jnp.int32, (ROWS, EXPERTS * CAP), 1)
    named = [ids_ref[:, k : k + 1] == lane // CAP for k in range(2)]
    has = (named[0] | named[1]).astype(F32)
    tri = lax.broadcasted_iota(jnp.int32, (ROWS, ROWS), 1) < lax.broadcasted_iota(jnp.int32, (ROWS, ROWS), 0)
    place = jnp.dot(tri.astype(F32).astype(BF16), has.astype(BF16), preferred_element_type=F32)
    here = place == (lane % CAP).astype(F32)
    return [(n & here).astype(F32) for n in named]


NB = 512
PG = 2
PC = D // PG
WL = D // NB


def project_kernel(
    o_ref, w_hbm, res_ref, gain_ref, ids_ref, e_in, arr_ref, hid_ref, e_ref,
    w, part, recv, norm, out, w_sem, rs_s, rs_r, a_s, a_r, f_s, f_r, snd, rcv, d_s, d_r,
):
    me, ex, x, z, core = place()
    sib = me + 1 - 2 * core

    def load(n):
        cols = pl.ds(pl.multiple_of(n * NB, NB), NB)
        return pltpu.make_async_copy(w_hbm.at[:, cols], w.at[n], w_sem.at[n])

    for n in range(WL):
        load(n).start()
    peers = [lax.rem(ex + d, EXP) for d in range(1, EXP)]
    greet(ring_peers() + [(sib, ex)] + [(me, p) for p in peers])
    start_hop(e_ref, PRE, ATTN_HOPS, snd, rcv, 0)
    start_hop(e_ref, DOWN, ATTN_DOWN, d_s, d_r, 0)

    def next_down(i):
        finish_hop(e_ref, DOWN, ATTN_DOWN + i, d_s, d_r, i)
        if i + 1 < PROJ_DOWN:
            start_hop(e_ref, DOWN, ATTN_DOWN + i + 1, d_s, d_r, i + 1)

    def next_hop(i):
        finish_hop(e_ref, PRE, ATTN_HOPS + i, snd, rcv, i)
        if i + 1 < PROJ_HOPS:
            start_hop(e_ref, PRE, ATTN_HOPS + i + 1, snd, rcv, i + 1)

    def share(g, d):
        p = lax.rem(ex + d, EXP)
        return remote(part.at[g, p], recv.at[g, d - 1], rs_s.at[g, d - 1], rs_r.at[g, d - 1], me, p)

    for g in range(PG):

        @pl.loop(0, PC // NB)
        def _(i):
            n = g * (PC // NB) + i
            load(n).wait()
            got = jnp.dot(o_ref[...], w[n], preferred_element_type=F32).astype(BF16)
            cols = pl.ds(pl.multiple_of(i * NB, NB), NB)
            for b in range(EXP):
                part[g, b, :, cols] = got[b * ROWS : (b + 1) * ROWS, :]

        for d in range(1, EXP):
            share(g, d).start()

    next_hop(0)
    for g in range(PG):
        if g == 0:
            next_hop(1)
            next_down(0)
        for d in range(1, EXP):
            share(g, d).wait_recv()

        @pl.loop(0, PC // NB)
        def _(i):
            cols = pl.ds(pl.multiple_of(i * NB, NB), NB)
            total = part[g, ex, :, cols].astype(F32)
            for d in range(EXP - 1):
                total += recv[g, d, :, cols].astype(F32)
            full = pl.ds(pl.multiple_of(g * PC + i * NB, NB), NB)
            hid_ref[:, full] = (res_ref[:, full].astype(F32) + total).astype(BF16)

    state = hid_ref[...].astype(F32)
    inv = 1.0 / jnp.sqrt(jnp.mean(state * state, axis=1, keepdims=True) + 1e-06)
    norm[...] = (state * inv * gain_ref[...].astype(F32)).astype(BF16)
    first, second = slots(ids_ref)
    table = (first + second).T.astype(BF16)
    out[...] = jnp.dot(table, norm[...], preferred_element_type=F32).astype(BF16).reshape(EXPERTS, CAP, D)

    def give_rows(d):
        p = lax.rem(ex + d, EXP)
        return remote(out.at[p], arr_ref.at[0, ex], a_s.at[d - 1], a_r.at[d - 1], me, p)

    def forward(d):
        source = lax.rem(ex + EXP - d, EXP)
        return remote(arr_ref.at[0, source], arr_ref.at[1, source], f_s.at[d], f_r.at[d], sib, ex)

    for d in range(1, EXP):
        give_rows(d).start()
    arr_ref[0, ex] = out[ex]
    forward(0).start()
    next_hop(2)
    for d in range(1, EXP):
        if d == EXP // 2:
            next_hop(3)
            next_down(1)
        source = lax.rem(ex + EXP - d, EXP)
        remote(out.at[ex], arr_ref.at[0, source], a_s.at[d - 1], a_r.at[d - 1], me, ex).wait_recv()
        forward(d).start()
    for d in range(EXP):
        forward(d).wait()
    next_hop(4)
    for d in range(1, EXP):
        for g in range(PG):
            share(g, d).wait_send()
        give_rows(d).wait_send()


def project(attn, w_out, residual, gain, ids, weights):
    dma = pltpu.SemaphoreType.DMA
    vmem, hbm = pl.BlockSpec(memory_space=pltpu.VMEM), pl.BlockSpec(memory_space=HBM)
    return pl.pallas_call(
        project_kernel,
        out_shape=(
            jax.ShapeDtypeStruct((NC, EXPERTS, CAP, D), BF16),
            jax.ShapeDtypeStruct((ROWS, D), BF16),
            WSHAPE,
        ),
        in_specs=[vmem, hbm, vmem, vmem, vmem, hbm],
        out_specs=(vmem, vmem, hbm),
        input_output_aliases={5: 2},
        scratch_shapes=[
            pltpu.VMEM((WL, HEADS * HD, NB), BF16),
            pltpu.VMEM((PG, EXP, ROWS, PC), BF16),
            pltpu.VMEM((PG, EXP - 1, ROWS, PC), BF16),
            pltpu.VMEM((ROWS, D), BF16),
            pltpu.VMEM((EXPERTS, CAP, D), BF16),
            dma((WL,)), dma((PG, EXP - 1)), dma((PG, EXP - 1)), dma((EXP - 1,)), dma((EXP - 1,)),
            dma((EXP,)), dma((EXP,)), dma((PROJ_HOPS, 2)), dma((PROJ_HOPS, 2)),
            dma((PROJ_DOWN, 2)), dma((PROJ_DOWN, 2)),
        ],
        compiler_params=pltpu.CompilerParams(collective_id=2, has_side_effects=True, vmem_limit_bytes=40 * MIB),
        cost_estimate=pl.CostEstimate(flops=2_200_000_000, bytes_accessed=64 * MIB, transcendentals=0),
        name="project_dispatch",
    )(attn, in_hbm(w_out), residual, gain, ids, in_hbm(weights))


SLOTS = EXPERTS * CAP
DEPTH = NC * 128
GCOLS = NC * DEPTH


def expert_kernel(
    arr_ref, w_in, hid_ref, ids_ref, gates_ref, o_ref, w_hbm,
    w, pre, act, mine, theirs, other, res, got, p_sem, d_sem, x_s, x_r, r_s, r_r, snd, rcv, d_s, d_r,
):
    me, ex, x, z, core = place()
    sib = me + 1 - 2 * core
    held = ATTN_HOPS + PROJ_HOPS + 1

    def at(step, way):
        return chip(x, z - step) if way == 0 else chip(1 - x, z + step)

    def load(kind, sem, step, way):
        c = at(step, way)
        return pltpu.make_async_copy(w_hbm.at[c, :, kind], w.at[c, :, kind], sem.at[step, way])

    for step in range(held):
        for way in range(2):
            load(PRE, p_sem, step, way).start()
    for step in range(DOWN_HELD):
        for way in range(2):
            load(DOWN, d_sem, step, way).start()
    peers = [lax.rem(ex + d, EXP) for d in range(1, EXP)]
    greet(ring_peers() + [(sib, ex)] + [(me, p) for p in peers])
    start_hop(w_hbm, PRE, held - 1, snd, rcv, 0)
    start_hop(w_hbm, DOWN, DOWN_HELD - 1, d_s, d_r, 0)
    pre[...] = jnp.zeros_like(pre)

    def use(step):
        for way in range(2):
            load(PRE, p_sem, step, way).wait()
            j = at(step, way)
            cols = pl.ds(pl.multiple_of(j * DEPTH, DEPTH), DEPTH)
            rows = arr_ref[:, :, :, cols].reshape(NC * SLOTS, DEPTH)
            tiles = [
                jnp.concatenate([w[j, c, pl.ds(t * 128, 128)] for c in range(NC)], axis=0) for t in range(2 * TILES)
            ]
            pre[...] += jnp.dot(rows, jnp.concatenate(tiles, axis=1), preferred_element_type=F32)

    def next_down(i):
        slot = i - DOWN_HELD + 1
        finish_hop(w_hbm, DOWN, i, d_s, d_r, slot)
        if i + 1 < NZ - 1:
            start_hop(w_hbm, DOWN, i + 1, d_s, d_r, slot + 1)
        for way in range(2):
            load(DOWN, d_sem, i + 1, way).start()

    @pl.loop(0, held)
    def _(step):
        use(step)

    next_down(DOWN_HELD - 1)
    for i in range(EXPERT_HOPS):
        finish_hop(w_hbm, PRE, held - 1 + i, snd, rcv, i)
        if i + 1 < EXPERT_HOPS:
            start_hop(w_hbm, PRE, held + i, snd, rcv, i + 1)
        for way in range(2):
            load(PRE, p_sem, held + i, way).start()
        use(held + i)

    gate = pre[:, :FH]
    act[...] = (gate / (1.0 + jnp.exp(-gate)) * pre[:, FH:]).astype(BF16)

    def swap(t):
        return remote(theirs.at[t], other.at[t], x_s.at[t], x_r.at[t], sib, ex)

    def give(t, d):
        p = lax.rem(ex + d, EXP)
        return remote(res.at[t, p], got.at[t, ex], r_s.at[t, d - 1], r_r.at[t, d - 1], me, p)

    def finish(t):
        swap(t).wait_recv()
        res[t] = (mine[t] + other[t]).astype(BF16).reshape(EXPERTS, CAP, GCOLS)
        for d in range(1, EXP):
            give(t, d).start()
        got[t, ex] = res[t, ex]

    first, second = slots(ids_ref)
    picks = jnp.concatenate([first, second], axis=0).astype(BF16)
    weight = [gates_ref[:, k : k + 1] for k in range(2)]

    def combine(t):
        for d in range(1, EXP):
            source = lax.rem(ex + EXP - d, EXP)
            remote(res.at[t, ex], got.at[t, source], r_s.at[t, d - 1], r_r.at[t, d - 1], me, ex).wait_recv()
        both = jnp.dot(picks, got[t].reshape(SLOTS, GCOLS), preferred_element_type=F32)
        total = weight[0] * both[:ROWS] + weight[1] * both[ROWS:]
        for way in range(2):
            cols = pl.ds(pl.multiple_of(at(t, way) * DEPTH, DEPTH), DEPTH)
            part = total[:, way * DEPTH : (way + 1) * DEPTH]
            o_ref[:, cols] = (hid_ref[:, cols].astype(F32) + part).astype(BF16)

    for t in range(NZ):
        if t in TAKEN:
            next_down(DOWN_HELD + TAKEN.index(t))
        for way in range(2):
            load(DOWN, d_sem, t, way).wait()
            down = jnp.concatenate([w[at(t, way), c, DOWN] for c in range(NC)], axis=1)
            made = jnp.dot(act[...], down, preferred_element_type=F32)
            mine[t, :, way * DEPTH : (way + 1) * DEPTH] = made[:SLOTS]
            theirs[t, :, way * DEPTH : (way + 1) * DEPTH] = made[SLOTS:]
        swap(t).start()
        if t >= 1:
            finish(t - 1)
        if t >= LAG:
            combine(t - LAG)
    finish(NZ - 1)
    for t in range(NZ - LAG, NZ):
        combine(t)
    for t in range(NZ):
        swap(t).wait_send()
        for d in range(1, EXP):
            give(t, d).wait_send()


LAG = 4
TAKEN = (1, 3, 6)


def experts(arrived, weights, hidden, ids, gates):
    vmem, hbm = pl.BlockSpec(memory_space=pltpu.VMEM), pl.BlockSpec(memory_space=HBM)
    return pl.pallas_call(
        expert_kernel,
        out_shape=(jax.ShapeDtypeStruct((ROWS, D), BF16), WSHAPE),
        in_specs=[vmem, hbm, vmem, vmem, vmem],
        out_specs=(vmem, hbm),
        input_output_aliases={1: 1},
        scratch_shapes=[
            pltpu.VMEM((CHIPS, NC, 3 * FH, 128), BF16),
            pltpu.VMEM((NC * SLOTS, 2 * FH), F32),
            pltpu.VMEM((NC * SLOTS, FH), BF16),
            pltpu.VMEM((NZ, SLOTS, GCOLS), F32),
            pltpu.VMEM((NZ, SLOTS, GCOLS), F32),
            pltpu.VMEM((NZ, SLOTS, GCOLS), F32),
            pltpu.VMEM((NZ, EXPERTS, CAP, GCOLS), BF16),
            pltpu.VMEM((NZ, EXPERTS, CAP, GCOLS), BF16),
            pltpu.SemaphoreType.DMA((NZ, 2)),
            pltpu.SemaphoreType.DMA((NZ, 2)),
            pltpu.SemaphoreType.DMA((NZ,)),
            pltpu.SemaphoreType.DMA((NZ,)),
            pltpu.SemaphoreType.DMA((NZ, EXP - 1)),
            pltpu.SemaphoreType.DMA((NZ, EXP - 1)),
            pltpu.SemaphoreType.DMA((EXPERT_HOPS, 2)),
            pltpu.SemaphoreType.DMA((EXPERT_HOPS, 2)),
            pltpu.SemaphoreType.DMA((NZ - DOWN_HELD, 2)),
            pltpu.SemaphoreType.DMA((NZ - DOWN_HELD, 2)),
        ],
        compiler_params=pltpu.CompilerParams(collective_id=3, has_side_effects=True, vmem_limit_bytes=48 * MIB),
        cost_estimate=pl.CostEstimate(flops=2_500_000_000, bytes_accessed=32 * MIB, transcendentals=100_000),
        name="experts",
    )(arrived, in_hbm(weights), hidden, ids, gates)[0]


def body(queries, keys, values, w_out, residual, norm_gain, expert_ids, gate_weights, w_gate, w_up, w_down):
    attn, weights = attention(queries, keys, values, w_gate[0], w_up[0], w_down[0])
    arrived, hidden, weights = project(attn, w_out, residual, norm_gain.reshape(1, D), expert_ids, weights)
    return experts(arrived, weights, hidden, expert_ids, gate_weights)


def solution(mesh):
    placed = (
        P("ctx", "exp"),
        P("ctx", None),
        P("ctx", None),
        P("exp", None),
        P(("ctx", "exp"), None),
        P(),
        P(("ctx", "exp"), None),
        P(("ctx", "exp"), None),
        P("exp", "ctx", None),
        P("exp", "ctx", None),
        P("exp", None, "ctx"),
    )
    return jax.shard_map(
        body, mesh=mesh, in_specs=placed, out_specs=P(("ctx", "exp"), None), check_vma=False
    )
```

```python
import functools
import math

import jax
import jax.numpy as jnp
from jax import lax
from jax.experimental import pallas as pl
from jax.experimental.pallas import tpu as pltpu
from jax.sharding import PartitionSpec as P

D = 4096
HQ = 64
KVH = 4
HD = 128
FF = 768
EXPERTS = 8
CAP = 16
ROWS = 32
NX, NZ, NC = 2, 8, 2
CTX = NX * NZ * NC
EXP = 8
TOK = 256
HALF = 128
HEADS = HQ // EXP
MESH = pl.DeviceIdType.MESH
MIB = 1 << 20
F32 = jnp.float32
BF16 = jnp.bfloat16


def remote(src, dst, send, recv, ctx, exp):
    return pltpu.make_async_remote_copy(
        src_ref=src, dst_ref=dst, send_sem=send, recv_sem=recv, device_id=(ctx, exp), device_id_type=MESH
    )


def greet(peers):
    barrier = pltpu.get_barrier_semaphore()
    for ctx, exp in peers:
        pl.semaphore_signal(barrier, inc=1, device_id=(ctx, exp), device_id_type=MESH)
    pl.semaphore_wait(barrier, len(peers))


def place():
    me = lax.axis_index("ctx")
    return me, lax.axis_index("exp"), me // (NZ * NC), (me // NC) % NZ, me % NC


def chunk(x, z, core):
    return x * (NZ * NC) + lax.rem(z + 2 * NZ, NZ) * NC + core


def chip(x, z):
    return x * NZ + lax.rem(z + 2 * NZ, NZ)


def hop_copies(w_ref, kind, hop, snd, rcv, slot):
    me, ex, x, z, core = place()
    out = []
    for way, (xx, step) in enumerate(((x, 1), (1 - x, -1))):
        ref = w_ref.at[chip(xx, z - step * hop), :, kind]
        out.append(remote(ref, ref, snd.at[slot, way], rcv.at[slot, way], chunk(x, z + step, core), ex))
    return out


def start_hop(*a):
    for c in hop_copies(*a):
        c.start()


def finish_hop(w_ref, kind, hop, snd, rcv, slot):
    me, ex, x, z, core = place()
    for way, (xx, step) in enumerate(((x, 1), (1 - x, -1))):
        ref = w_ref.at[chip(xx, z - step * (hop + 1)), :, kind]
        remote(ref, ref, snd.at[slot, way], rcv.at[slot, way], me, ex).wait_recv()
    for c in hop_copies(w_ref, kind, hop, snd, rcv, slot):
        c.wait_send()


def down_piece(w_ref, xx, step, way):
    me, ex, x, z, core = place()
    return w_ref.at[chip(xx, z - step if way == 0 else z + step), way, DOWN]


def down_hop(w_ref, hop, way, snd, rcv, slot):
    me, ex, x, z, core = place()
    ref = down_piece(w_ref, x, hop, way)
    return remote(ref, ref, snd.at[slot, way], rcv.at[slot, way], chunk(x, z + (1 if way == 0 else -1), core), ex)


def down_cross(w_ref, hop, way, snd, rcv, slot):
    me, ex, x, z, core = place()
    ref = down_piece(w_ref, x, hop + 1, way)
    return remote(ref, ref, snd.at[slot, way], rcv.at[slot, way], chunk(1 - x, z, core), ex)


def start_down(w_ref, hop, snd, rcv, slot):
    for way in range(2):
        down_hop(w_ref, hop, way, snd, rcv, slot).start()


def pass_down(w_ref, hop, snd, rcv, c_s, c_r, slot, last):
    me, ex, x, z, core = place()
    for way in range(2):
        ref = down_piece(w_ref, x, hop + 1, way)
        remote(ref, ref, snd.at[slot, way], rcv.at[slot, way], me, ex).wait_recv()
    if not last:
        start_down(w_ref, hop + 1, snd, rcv, slot + 1)
    for way in range(2):
        down_cross(w_ref, hop, way, c_s, c_r, slot).start()


def crossed(w_ref, hop, c_s, c_r, slot):
    me, ex, x, z, core = place()
    for way in range(2):
        ref = down_piece(w_ref, 1 - x, hop + 1, way)
        remote(ref, ref, c_s.at[slot, way], c_r.at[slot, way], me, ex).wait_recv()


def sent_down(w_ref, hop, snd, rcv, c_s, c_r, slot):
    for way in range(2):
        down_hop(w_ref, hop, way, snd, rcv, slot).wait_send()
        down_cross(w_ref, hop, way, c_s, c_r, slot).wait_send()


def ring_peers():
    me, ex, x, z, core = place()
    return [(chunk(x, z + 1, core), ex), (chunk(x, z - 1, core), ex), (chunk(1 - x, z, core), ex)]


HBM = pltpu.HBM
TILES = FF // NC // 128
FH = FF // NC
CHIPS = CTX // NC
WSHAPE = HBM((CHIPS, NC, 3 * FH, 128), BF16)


def in_hbm(x):
    return pltpu.with_memory_space_constraint(x, HBM)


PRE, DOWN = pl.ds(0, 2 * FH), pl.ds(2 * FH, FH)
ATTN_HOPS, PROJ_HOPS = 1, 5
ATTN_DOWN, PROJ_DOWN = 1, 2
EXPERT_HOPS = NZ - 1 - ATTN_HOPS - PROJ_HOPS
DOWN_HELD = ATTN_DOWN + PROJ_DOWN + 1


CK = NC * TOK
KB = 2 * CK
TR = 128
QROWS = HEADS * HALF
SCALE2 = math.log2(math.e) / math.sqrt(HD)
NP = 2 * TILES + 1


def attn_kernel(
    q_ref, k_ref, v_ref, g_ref, u_ref, d_ref, o_ref, w_ref,
    kv, qs, acc, m_sc, vx,
    kv_l, q_l, own_s, own_r, ring_s, ring_r, sib_s, sib_r, w_l, w_s, w_r, wx_s, wx_r, snd, rcv, d_s, d_r, c_s, c_r,
):
    me, ex, x, z, core = place()
    up, down = chunk(x, z + 1, core), chunk(x, z - 1, core)
    across, sib = chunk(1 - x, z, core), chunk(x, z, 1 - core)
    here = chip(x, z)
    head = pl.ds(pl.multiple_of((ex // 2) * HD, HD), HD)

    def part(c, cc):
        return kv.at[c, :, pl.ds(pl.multiple_of(cc * TOK, TOK), TOK)]

    def pieces(half):
        for a, ref in enumerate((g_ref, u_ref)):
            for t in range(TILES):
                cols = pl.ds(pl.multiple_of(half * FH + t * 128, 128), 128)
                yield ref.at[:, cols], w_ref.at[here, core, pl.ds((a * TILES + t) * 128, 128)]
        yield d_ref.at[pl.ds(pl.multiple_of(half * FH, FH), FH)], w_ref.at[here, core, pl.ds(2 * FH, FH)]

    rows0 = pl.ds(pl.multiple_of(core * TOK, TOK), TOK)
    kvl = [
        pltpu.make_async_copy(ref.at[:, head], kv.at[here, i, rows0], kv_l.at[i]) for i, ref in enumerate((k_ref, v_ref))
    ]
    ql = [
        pltpu.make_async_copy(
            q_ref.at[pl.ds(a * HALF, HALF), pl.ds(h * HD, HD)], qs.at[a, pl.ds(h * HALF, HALF)], q_l.at[a, h]
        )
        for a in range(2)
        for h in range(HEADS)
    ]
    kept = [pltpu.make_async_copy(src, dst, w_l.at[i]) for i, (src, dst) in enumerate(pieces(core))]
    for c in kvl + ql + kept:
        c.start()
    greet([(up, ex), (down, ex), (across, ex), (sib, ex)])
    for c in kvl:
        c.wait()

    def piece(way, step, cc):
        return part(chip(x, z - step) if way == 0 else chip(1 - x, z + step), cc)

    def hop(way, step):
        ref = piece(way, step, core)
        return remote(ref, ref, ring_s.at[way, step], ring_r.at[way, step], up if way == 0 else down, ex)

    def share(way, step):
        ref = piece(way, step, core)
        return remote(ref, ref, sib_s.at[way, step], sib_r.at[way, step], sib, ex)

    def shared(way, step):
        ref = piece(way, step, 1 - core)
        remote(ref, ref, sib_s.at[way, step], sib_r.at[way, step], me, ex).wait_recv()

    own = part(here, core)
    cross = remote(own, own, own_s, own_r, across, ex)
    cross.start()
    hop(0, 0).start()
    share(0, 0).start()
    other = part(chip(1 - x, z), core)
    remote(other, other, own_s, own_r, me, ex).wait_recv()
    hop(1, 0).start()
    share(1, 0).start()
    wsent = [remote(src, dst, w_s.at[i], w_r.at[i], sib, ex) for i, (src, dst) in enumerate(pieces(1 - core))]
    for c in wsent:
        c.start()
    wcross = remote(w_ref.at[here], w_ref.at[here], wx_s, wx_r, across, ex)
    vx[:, HD:] = jnp.ones((KB, HD), BF16)
    m_sc[...] = jnp.full_like(m_sc, -1e30)
    acc[...] = jnp.zeros_like(acc)
    for c in ql:
        c.wait()

    def block(which, start, c0, c1, masked):
        k = jnp.concatenate([kv[c0, 0], kv[c1, 0]], axis=0)
        for t in range(QROWS // TR):
            rows = pl.ds(t * TR, TR)
            s = lax.dot_general(qs[which, rows, :], k, (((1,), (1,)), ((), ())), preferred_element_type=F32)
            if masked:
                row = lax.broadcasted_iota(jnp.int32, (TR, KB), 0) % HALF + start
                lane = lax.broadcasted_iota(jnp.int32, (TR, KB), 1)
                col = lane + jnp.where(lane < CK, c0 * CK, c1 * CK - CK)
                s = jnp.where(col <= row, s, -1e30)
            old = m_sc[which, rows, :]
            new = jnp.maximum(old, jnp.max(s, axis=1, keepdims=True))
            p = jnp.exp2((s - new[:, :1]) * SCALE2)
            factor = jnp.exp2((old - new) * SCALE2)
            m_sc[which, rows, :] = new
            acc[which, rows, :] = acc[which, rows, :] * jnp.concatenate([factor, factor], axis=1) + jnp.dot(
                p.astype(BF16), vx[...], preferred_element_type=F32
            )

    @pl.loop(0, NZ + 1)
    def _(u):
        step = u + 1

        @pl.when(step < NZ)
        def _():
            for way in range(2):
                ref = piece(way, step, core)
                remote(ref, ref, ring_s.at[way, step - 1], ring_r.at[way, step - 1], me, ex).wait_recv()

                @pl.when(step < NZ - 1)
                def _():
                    hop(way, step).start()

                share(way, step).start()

        @pl.when(u == 2)
        def _():
            for i in range(NP):
                kept[i].wait()
                wsent[i].wait_recv()
            wcross.start()

        @pl.when(u == NZ - 2)
        def _():
            wcross.wait_recv()
            start_hop(w_ref, PRE, 0, snd, rcv, 0)
            start_down(w_ref, 0, d_s, d_r, 0)

        @pl.when(u == NZ)
        def _():
            pass_down(w_ref, 0, d_s, d_r, c_s, c_r, 0, True)

        turn = u - 1
        way = lax.rem(turn + 2, 2)
        pair = turn - way

        @pl.when(turn >= 0)
        def _():
            mine = way == 0
            for w in range(2):

                @pl.when(way == w)
                def _():
                    shared(w, pair)
                    shared(w, pair + 1)

            c0 = jnp.where(mine, chip(x, z - pair), chip(1 - x, z + pair))
            c1 = jnp.where(mine, chip(x, z - pair - 1), chip(1 - x, z + pair + 1))
            vx[pl.ds(0, CK), :HD] = kv[c0, 1]
            vx[pl.ds(CK, CK), :HD] = kv[c1, 1]

            @pl.loop(0, 2)
            def _(which):
                start = me * TOK + which * HALF
                full = jnp.maximum(c0, c1) * CK + CK - 1 <= start
                some = jnp.minimum(c0, c1) * CK <= start

                @pl.when(full)
                def _():
                    block(which, start, c0, c1, False)

                @pl.when(some & jnp.logical_not(full))
                def _():
                    block(which, start, c0, c1, True)

    for which in range(2):
        for h in range(HEADS):
            rows = pl.ds(h * HALF, HALF)
            made = (acc[which, rows, :HD] / acc[which, rows, HD:]).astype(BF16)
            o_ref[pl.ds(which * HALF, HALF), pl.ds(h * HD, HD)] = made
    finish_hop(w_ref, PRE, 0, snd, rcv, 0)
    crossed(w_ref, 0, c_s, c_r, 0)
    sent_down(w_ref, 0, d_s, d_r, c_s, c_r, 0)
    cross.wait_send()
    wcross.wait_send()
    for c in wsent:
        c.wait_send()
    for way in range(2):
        for step in range(NZ):
            share(way, step).wait_send()
            if step < NZ - 1:
                hop(way, step).wait_send()


def attention(queries, keys, values, w_gate, w_up, w_down):
    dma = pltpu.SemaphoreType.DMA
    hbm = pl.BlockSpec(memory_space=HBM)
    return pl.pallas_call(
        attn_kernel,
        out_shape=(jax.ShapeDtypeStruct((TOK, HEADS * HD), BF16), WSHAPE),
        in_specs=[hbm] * 6,
        out_specs=(pl.BlockSpec(memory_space=pltpu.VMEM), hbm),
        scratch_shapes=[
            pltpu.VMEM((CHIPS, 2, CK, HD), BF16),
            pltpu.VMEM((2, QROWS, HD), BF16),
            pltpu.VMEM((2, QROWS, 2 * HD), F32),
            pltpu.VMEM((2, QROWS, HD), F32),
            pltpu.VMEM((KB, 2 * HD), BF16),
            dma((2,)), dma((2, HEADS)),
            dma, dma,
            dma((2, NZ - 1)), dma((2, NZ - 1)), dma((2, NZ)), dma((2, NZ)),
            dma((NP,)), dma((NP,)), dma((NP,)), dma, dma,
            dma((ATTN_HOPS, 2)), dma((ATTN_HOPS, 2)), dma((ATTN_DOWN, 2)), dma((ATTN_DOWN, 2)),
            dma((ATTN_DOWN, 2)), dma((ATTN_DOWN, 2)),
        ],
        compiler_params=pltpu.CompilerParams(collective_id=1, has_side_effects=True, vmem_limit_bytes=32 * MIB),
        cost_estimate=pl.CostEstimate(flops=9_000_000_000, bytes_accessed=64 * MIB, transcendentals=9_000_000),
        name="attention",
    )(*(in_hbm(a) for a in (queries, keys, values, w_gate, w_up, w_down)))


def slots(ids_ref):
    lane = lax.broadcasted_iota(jnp.int32, (ROWS, EXPERTS * CAP), 1)
    named = [ids_ref[:, k : k + 1] == lane // CAP for k in range(2)]
    has = (named[0] | named[1]).astype(F32)
    tri = lax.broadcasted_iota(jnp.int32, (ROWS, ROWS), 1) < lax.broadcasted_iota(jnp.int32, (ROWS, ROWS), 0)
    place = jnp.dot(tri.astype(F32).astype(BF16), has.astype(BF16), preferred_element_type=F32)
    here = place == (lane % CAP).astype(F32)
    return [(n & here).astype(F32) for n in named]


NB = 512
PG = 2
PC = D // PG
WL = D // NB


def project_kernel(
    o_ref, w_hbm, res_ref, gain_ref, ids_ref, e_in, arr_ref, hid_ref, e_ref,
    w, part, recv, norm, out, w_sem, rs_s, rs_r, a_s, a_r, f_s, f_r, snd, rcv, d_s, d_r, c_s, c_r,
):
    me, ex, x, z, core = place()
    sib = me + 1 - 2 * core

    def load(n):
        cols = pl.ds(pl.multiple_of(n * NB, NB), NB)
        return pltpu.make_async_copy(w_hbm.at[:, cols], w.at[n], w_sem.at[n])

    for n in range(WL):
        load(n).start()
    peers = [lax.rem(ex + d, EXP) for d in range(1, EXP)]
    greet(ring_peers() + [(sib, ex)] + [(me, p) for p in peers])
    start_hop(e_ref, PRE, ATTN_HOPS, snd, rcv, 0)
    start_down(e_ref, ATTN_DOWN, d_s, d_r, 0)

    def next_down(i):
        pass_down(e_ref, ATTN_DOWN + i, d_s, d_r, c_s, c_r, i, i + 1 == PROJ_DOWN)

    def next_hop(i):
        finish_hop(e_ref, PRE, ATTN_HOPS + i, snd, rcv, i)
        if i + 1 < PROJ_HOPS:
            start_hop(e_ref, PRE, ATTN_HOPS + i + 1, snd, rcv, i + 1)

    def share(g, d):
        p = lax.rem(ex + d, EXP)
        return remote(part.at[g, p], recv.at[g, d - 1], rs_s.at[g, d - 1], rs_r.at[g, d - 1], me, p)

    for g in range(PG):

        @pl.loop(0, PC // NB)
        def _(i):
            n = g * (PC // NB) + i
            load(n).wait()
            got = jnp.dot(o_ref[...], w[n], preferred_element_type=F32).astype(BF16)
            cols = pl.ds(pl.multiple_of(i * NB, NB), NB)
            for b in range(EXP):
                part[g, b, :, cols] = got[b * ROWS : (b + 1) * ROWS, :]

        for d in range(1, EXP):
            share(g, d).start()

    next_hop(0)
    for g in range(PG):
        if g == 0:
            next_hop(1)
            next_down(0)
        for d in range(1, EXP):
            share(g, d).wait_recv()

        @pl.loop(0, PC // NB)
        def _(i):
            cols = pl.ds(pl.multiple_of(i * NB, NB), NB)
            total = part[g, ex, :, cols].astype(F32)
            for d in range(EXP - 1):
                total += recv[g, d, :, cols].astype(F32)
            full = pl.ds(pl.multiple_of(g * PC + i * NB, NB), NB)
            hid_ref[:, full] = (res_ref[:, full].astype(F32) + total).astype(BF16)

    state = hid_ref[...].astype(F32)
    inv = 1.0 / jnp.sqrt(jnp.mean(state * state, axis=1, keepdims=True) + 1e-06)
    norm[...] = (state * inv * gain_ref[...].astype(F32)).astype(BF16)
    first, second = slots(ids_ref)
    table = (first + second).T.astype(BF16)
    out[...] = jnp.dot(table, norm[...], preferred_element_type=F32).astype(BF16).reshape(EXPERTS, CAP, D)

    def give_rows(d):
        p = lax.rem(ex + d, EXP)
        return remote(out.at[p], arr_ref.at[0, ex], a_s.at[d - 1], a_r.at[d - 1], me, p)

    def forward(d):
        source = lax.rem(ex + EXP - d, EXP)
        return remote(arr_ref.at[0, source], arr_ref.at[1, source], f_s.at[d], f_r.at[d], sib, ex)

    for d in range(1, EXP):
        give_rows(d).start()
    arr_ref[0, ex] = out[ex]
    forward(0).start()
    next_hop(2)
    for d in range(1, EXP):
        if d == EXP // 2:
            next_hop(3)
            next_down(1)
        source = lax.rem(ex + EXP - d, EXP)
        remote(out.at[ex], arr_ref.at[0, source], a_s.at[d - 1], a_r.at[d - 1], me, ex).wait_recv()
        forward(d).start()
    for d in range(EXP):
        forward(d).wait()
    next_hop(4)
    for i in range(PROJ_DOWN):
        crossed(e_ref, ATTN_DOWN + i, c_s, c_r, i)
        sent_down(e_ref, ATTN_DOWN + i, d_s, d_r, c_s, c_r, i)
    for d in range(1, EXP):
        for g in range(PG):
            share(g, d).wait_send()
        give_rows(d).wait_send()


def project(attn, w_out, residual, gain, ids, weights):
    dma = pltpu.SemaphoreType.DMA
    vmem, hbm = pl.BlockSpec(memory_space=pltpu.VMEM), pl.BlockSpec(memory_space=HBM)
    return pl.pallas_call(
        project_kernel,
        out_shape=(
            jax.ShapeDtypeStruct((NC, EXPERTS, CAP, D), BF16),
            jax.ShapeDtypeStruct((ROWS, D), BF16),
            WSHAPE,
        ),
        in_specs=[vmem, hbm, vmem, vmem, vmem, hbm],
        out_specs=(vmem, vmem, hbm),
        input_output_aliases={5: 2},
        scratch_shapes=[
            pltpu.VMEM((WL, HEADS * HD, NB), BF16),
            pltpu.VMEM((PG, EXP, ROWS, PC), BF16),
            pltpu.VMEM((PG, EXP - 1, ROWS, PC), BF16),
            pltpu.VMEM((ROWS, D), BF16),
            pltpu.VMEM((EXPERTS, CAP, D), BF16),
            dma((WL,)), dma((PG, EXP - 1)), dma((PG, EXP - 1)), dma((EXP - 1,)), dma((EXP - 1,)),
            dma((EXP,)), dma((EXP,)), dma((PROJ_HOPS, 2)), dma((PROJ_HOPS, 2)),
            dma((PROJ_DOWN, 2)), dma((PROJ_DOWN, 2)), dma((PROJ_DOWN, 2)), dma((PROJ_DOWN, 2)),
        ],
        compiler_params=pltpu.CompilerParams(collective_id=2, has_side_effects=True, vmem_limit_bytes=40 * MIB),
        cost_estimate=pl.CostEstimate(flops=2_200_000_000, bytes_accessed=64 * MIB, transcendentals=0),
        name="project_dispatch",
    )(attn, in_hbm(w_out), residual, gain, ids, in_hbm(weights))


SLOTS = EXPERTS * CAP
DEPTH = NC * 128
GCOLS = NC * DEPTH


def expert_kernel(
    arr_ref, w_in, hid_ref, ids_ref, gates_ref, o_ref, w_hbm,
    w, pre, act, mine, theirs, other, res, got, p_sem, d_sem, x_s, x_r, r_s, r_r, snd, rcv, d_s, d_r, c_s, c_r,
):
    me, ex, x, z, core = place()
    sib = me + 1 - 2 * core
    held = ATTN_HOPS + PROJ_HOPS + 1

    def at(step, way):
        return chip(x, z - step) if way == 0 else chip(1 - x, z + step)

    def load(step, way):
        c = at(step, way)
        return pltpu.make_async_copy(w_hbm.at[c, :, PRE], w.at[c, :, PRE], p_sem.at[step, way])

    def where(step, k):
        way = k % 2
        return chip(x if k < 2 else 1 - x, z - step if way == 0 else z + step), way

    def load_down(step, k):
        c, way = where(step, k)
        return pltpu.make_async_copy(w_hbm.at[c, way, DOWN], w.at[c, way, DOWN], d_sem.at[step, k])

    for step in range(held):
        for way in range(2):
            load(step, way).start()
    for step in range(DOWN_HELD):
        for k in range(4):
            load_down(step, k).start()
    peers = [lax.rem(ex + d, EXP) for d in range(1, EXP)]
    greet(ring_peers() + [(sib, ex)] + [(me, p) for p in peers])
    start_hop(w_hbm, PRE, held - 1, snd, rcv, 0)
    start_down(w_hbm, DOWN_HELD - 1, d_s, d_r, 0)
    pre[...] = jnp.zeros_like(pre)

    def use(step):
        for way in range(2):
            load(step, way).wait()
            j = at(step, way)
            cols = pl.ds(pl.multiple_of(j * DEPTH, DEPTH), DEPTH)
            rows = arr_ref[:, :, :, cols].reshape(NC * SLOTS, DEPTH)
            tiles = [
                jnp.concatenate([w[j, c, pl.ds(t * 128, 128)] for c in range(NC)], axis=0) for t in range(2 * TILES)
            ]
            pre[...] += jnp.dot(rows, jnp.concatenate(tiles, axis=1), preferred_element_type=F32)

    def next_down(i):
        pass_down(w_hbm, i, d_s, d_r, c_s, c_r, i - DOWN_HELD + 1, i + 1 == NZ - 1)
        for k in range(2):
            load_down(i + 1, k).start()

    def take_cross(i):
        crossed(w_hbm, i, c_s, c_r, i - DOWN_HELD + 1)
        for k in range(2, 4):
            load_down(i + 1, k).start()

    @pl.loop(0, held)
    def _(step):
        use(step)

    next_down(DOWN_HELD - 1)
    for i in range(EXPERT_HOPS):
        finish_hop(w_hbm, PRE, held - 1 + i, snd, rcv, i)
        if i + 1 < EXPERT_HOPS:
            start_hop(w_hbm, PRE, held + i, snd, rcv, i + 1)
        for way in range(2):
            load(held + i, way).start()
        if i == 0:
            next_down(DOWN_HELD)
        use(held + i)
    take_cross(DOWN_HELD - 1)

    gate = pre[:, :FH]
    act[...] = (gate / (1.0 + jnp.exp(-gate)) * pre[:, FH:]).astype(BF16)

    def swap(t):
        return remote(theirs.at[t], other.at[t], x_s.at[t], x_r.at[t], sib, ex)

    def give(t, d):
        p = lax.rem(ex + d, EXP)
        return remote(res.at[t, p], got.at[t, ex], r_s.at[t, d - 1], r_r.at[t, d - 1], me, p)

    def finish(t):
        swap(t).wait_recv()
        res[t] = (mine[t] + other[t]).astype(BF16).reshape(EXPERTS, CAP, GCOLS)
        for d in range(1, EXP):
            give(t, d).start()
        got[t, ex] = res[t, ex]

    first, second = slots(ids_ref)
    picks = jnp.concatenate([first, second], axis=0).astype(BF16)
    weight = [gates_ref[:, k : k + 1] for k in range(2)]

    def combine(t):
        for d in range(1, EXP):
            source = lax.rem(ex + EXP - d, EXP)
            remote(res.at[t, ex], got.at[t, source], r_s.at[t, d - 1], r_r.at[t, d - 1], me, ex).wait_recv()
        both = jnp.dot(picks, got[t].reshape(SLOTS, GCOLS), preferred_element_type=F32)
        total = weight[0] * both[:ROWS] + weight[1] * both[ROWS:]
        for k in range(4):
            c, way = where(t, k)
            cols = pl.ds(pl.multiple_of(c * DEPTH + way * 128, 128), 128)
            o_ref[:, cols] = (hid_ref[:, cols].astype(F32) + total[:, k * 128 : (k + 1) * 128]).astype(BF16)

    for t in range(NZ):
        if t == 1:
            next_down(DOWN_HELD + 1)
            take_cross(DOWN_HELD)
        if t == 3:
            next_down(DOWN_HELD + 2)
            take_cross(DOWN_HELD + 1)
        if t == 5:
            take_cross(DOWN_HELD + 2)
        for k in range(4):
            load_down(t, k).wait()
        down = jnp.concatenate([w[where(t, k)[0], k % 2, DOWN] for k in range(4)], axis=1)
        made = jnp.dot(act[...], down, preferred_element_type=F32)
        mine[t] = made[:SLOTS]
        theirs[t] = made[SLOTS:]
        swap(t).start()
        if t >= 1:
            finish(t - 1)
        if t >= LAG:
            combine(t - LAG)
    finish(NZ - 1)
    for t in range(NZ - LAG, NZ):
        combine(t)
    for i in range(DOWN_HELD - 1, NZ - 1):
        sent_down(w_hbm, i, d_s, d_r, c_s, c_r, i - DOWN_HELD + 1)
    for t in range(NZ):
        swap(t).wait_send()
        for d in range(1, EXP):
            give(t, d).wait_send()


LAG = 4


def experts(arrived, weights, hidden, ids, gates):
    vmem, hbm = pl.BlockSpec(memory_space=pltpu.VMEM), pl.BlockSpec(memory_space=HBM)
    return pl.pallas_call(
        expert_kernel,
        out_shape=(jax.ShapeDtypeStruct((ROWS, D), BF16), WSHAPE),
        in_specs=[vmem, hbm, vmem, vmem, vmem],
        out_specs=(vmem, hbm),
        input_output_aliases={1: 1},
        scratch_shapes=[
            pltpu.VMEM((CHIPS, NC, 3 * FH, 128), BF16),
            pltpu.VMEM((NC * SLOTS, 2 * FH), F32),
            pltpu.VMEM((NC * SLOTS, FH), BF16),
            pltpu.VMEM((NZ, SLOTS, GCOLS), F32),
            pltpu.VMEM((NZ, SLOTS, GCOLS), F32),
            pltpu.VMEM((NZ, SLOTS, GCOLS), F32),
            pltpu.VMEM((NZ, EXPERTS, CAP, GCOLS), BF16),
            pltpu.VMEM((NZ, EXPERTS, CAP, GCOLS), BF16),
            pltpu.SemaphoreType.DMA((NZ, 2)),
            pltpu.SemaphoreType.DMA((NZ, 4)),
            pltpu.SemaphoreType.DMA((NZ,)),
            pltpu.SemaphoreType.DMA((NZ,)),
            pltpu.SemaphoreType.DMA((NZ, EXP - 1)),
            pltpu.SemaphoreType.DMA((NZ, EXP - 1)),
            pltpu.SemaphoreType.DMA((EXPERT_HOPS, 2)),
            pltpu.SemaphoreType.DMA((EXPERT_HOPS, 2)),
            pltpu.SemaphoreType.DMA((NZ - DOWN_HELD, 2)),
            pltpu.SemaphoreType.DMA((NZ - DOWN_HELD, 2)),
            pltpu.SemaphoreType.DMA((NZ - DOWN_HELD, 2)),
            pltpu.SemaphoreType.DMA((NZ - DOWN_HELD, 2)),
        ],
        compiler_params=pltpu.CompilerParams(collective_id=3, has_side_effects=True, vmem_limit_bytes=48 * MIB),
        cost_estimate=pl.CostEstimate(flops=2_500_000_000, bytes_accessed=32 * MIB, transcendentals=100_000),
        name="experts",
    )(arrived, in_hbm(weights), hidden, ids, gates)[0]


def body(queries, keys, values, w_out, residual, norm_gain, expert_ids, gate_weights, w_gate, w_up, w_down):
    attn, weights = attention(queries, keys, values, w_gate[0], w_up[0], w_down[0])
    arrived, hidden, weights = project(attn, w_out, residual, norm_gain.reshape(1, D), expert_ids, weights)
    return experts(arrived, weights, hidden, expert_ids, gate_weights)


def solution(mesh):
    placed = (
        P("ctx", "exp"),
        P("ctx", None),
        P("ctx", None),
        P("exp", None),
        P(("ctx", "exp"), None),
        P(),
        P(("ctx", "exp"), None),
        P(("ctx", "exp"), None),
        P("exp", "ctx", None),
        P("exp", "ctx", None),
        P("exp", None, "ctx"),
    )
    return jax.shard_map(
        body, mesh=mesh, in_specs=placed, out_specs=P(("ctx", "exp"), None), check_vma=False
    )
```

```python
import functools
import math

import jax
import jax.numpy as jnp
from jax import lax
from jax.experimental import pallas as pl
from jax.experimental.pallas import tpu as pltpu
from jax.sharding import PartitionSpec as P

D = 4096
HQ = 64
KVH = 4
HD = 128
FF = 768
EXPERTS = 8
CAP = 16
ROWS = 32
NX, NZ, NC = 2, 8, 2
CTX = NX * NZ * NC
EXP = 8
TOK = 256
HALF = 128
HEADS = HQ // EXP
MESH = pl.DeviceIdType.MESH
MIB = 1 << 20
F32 = jnp.float32
BF16 = jnp.bfloat16


def remote(src, dst, send, recv, ctx, exp):
    return pltpu.make_async_remote_copy(
        src_ref=src, dst_ref=dst, send_sem=send, recv_sem=recv, device_id=(ctx, exp), device_id_type=MESH
    )


def greet(peers):
    barrier = pltpu.get_barrier_semaphore()
    for ctx, exp in peers:
        pl.semaphore_signal(barrier, inc=1, device_id=(ctx, exp), device_id_type=MESH)
    pl.semaphore_wait(barrier, len(peers))


def place():
    me = lax.axis_index("ctx")
    return me, lax.axis_index("exp"), me // (NZ * NC), (me // NC) % NZ, me % NC


def chunk(x, z, core):
    return x * (NZ * NC) + lax.rem(z + 2 * NZ, NZ) * NC + core


def chip(x, z):
    return x * NZ + lax.rem(z + 2 * NZ, NZ)


def hop_copies(w_ref, kind, hop, snd, rcv, slot):
    me, ex, x, z, core = place()
    out = []
    for way, (xx, step) in enumerate(((x, 1), (1 - x, -1))):
        ref = w_ref.at[chip(xx, z - step * hop), :, kind]
        out.append(remote(ref, ref, snd.at[slot, way], rcv.at[slot, way], chunk(x, z + step, core), ex))
    return out


def start_hop(*a):
    for c in hop_copies(*a):
        c.start()


def finish_hop(w_ref, kind, hop, snd, rcv, slot):
    me, ex, x, z, core = place()
    for way, (xx, step) in enumerate(((x, 1), (1 - x, -1))):
        ref = w_ref.at[chip(xx, z - step * (hop + 1)), :, kind]
        remote(ref, ref, snd.at[slot, way], rcv.at[slot, way], me, ex).wait_recv()
    for c in hop_copies(w_ref, kind, hop, snd, rcv, slot):
        c.wait_send()


def ring_peers():
    me, ex, x, z, core = place()
    return [(chunk(x, z + 1, core), ex), (chunk(x, z - 1, core), ex)]


HBM = pltpu.HBM
TILES = FF // NC // 128
FH = FF // NC
CHIPS = CTX // NC
WSHAPE = HBM((CHIPS, NC, 3 * FH, 128), BF16)


def in_hbm(x):
    return pltpu.with_memory_space_constraint(x, HBM)


PRE, DOWN = pl.ds(0, 2 * FH), pl.ds(2 * FH, FH)
ATTN_HOPS, PROJ_HOPS = 1, 5
ATTN_DOWN, PROJ_DOWN = 1, 2
EXPERT_HOPS = NZ - 1 - ATTN_HOPS - PROJ_HOPS
DOWN_HELD = ATTN_DOWN + PROJ_DOWN + 1


CK = NC * TOK
KB = 2 * CK
TR = 128
QROWS = HEADS * HALF
SCALE2 = math.log2(math.e) / math.sqrt(HD)
NP = 2 * TILES + 1
FAR = NZ // 2


def attn_kernel(
    q_ref, k_ref, v_ref, g_ref, u_ref, d_ref, o_ref, w_ref,
    kv, qs, acc, m_sc, vx,
    kv_l, q_l, own_s, own_r, ring_s, ring_r, sib_s, sib_r, w_l, w_s, w_r, wx_s, wx_r, snd, rcv, d_s, d_r,
):
    me, ex, x, z, core = place()
    up, down = chunk(x, z + 1, core), chunk(x, z - 1, core)
    across, sib = chunk(1 - x, z, core), chunk(x, z, 1 - core)
    here = chip(x, z)
    head = pl.ds(pl.multiple_of((ex // 2) * HD, HD), HD)

    def part(c, cc):
        return kv.at[c, :, pl.ds(pl.multiple_of(cc * TOK, TOK), TOK)]

    def pieces(half):
        for a, ref in enumerate((g_ref, u_ref)):
            for t in range(TILES):
                cols = pl.ds(pl.multiple_of(half * FH + t * 128, 128), 128)
                yield ref.at[:, cols], w_ref.at[here, core, pl.ds((a * TILES + t) * 128, 128)]
        yield d_ref.at[pl.ds(pl.multiple_of(half * FH, FH), FH)], w_ref.at[here, core, pl.ds(2 * FH, FH)]

    rows0 = pl.ds(pl.multiple_of(core * TOK, TOK), TOK)
    kvl = [
        pltpu.make_async_copy(ref.at[:, head], kv.at[here, i, rows0], kv_l.at[i]) for i, ref in enumerate((k_ref, v_ref))
    ]
    ql = [
        pltpu.make_async_copy(
            q_ref.at[pl.ds(a * HALF, HALF), pl.ds(h * HD, HD)], qs.at[a, pl.ds(h * HALF, HALF)], q_l.at[a, h]
        )
        for a in range(2)
        for h in range(HEADS)
    ]
    kept = [pltpu.make_async_copy(src, dst, w_l.at[i]) for i, (src, dst) in enumerate(pieces(core))]
    for c in kvl + ql + kept:
        c.start()
    greet([(up, ex), (down, ex), (across, ex), (sib, ex)])
    for c in kvl:
        c.wait()

    def piece(flow, step, cc):
        return part(chip(x if flow in (0, 2) else 1 - x, z - step if flow in (0, 3) else z + step), cc)

    def hop(flow, step):
        ref = piece(flow, step, core)
        target = up if flow in (0, 3) else down
        return remote(ref, ref, ring_s.at[flow, step], ring_r.at[flow, step], target, ex)

    def share(flow, step):
        ref = piece(flow, step, core)
        return remote(ref, ref, sib_s.at[flow, step], sib_r.at[flow, step], sib, ex)

    def shared(way, step):
        ref = piece(way, step, 1 - core)
        remote(ref, ref, sib_s.at[way, step], sib_r.at[way, step], me, ex).wait_recv()

    own = part(here, core)
    cross = remote(own, own, own_s, own_r, across, ex)
    cross.start()
    hop(0, 0).start()
    hop(2, 0).start()
    share(0, 0).start()
    other = part(chip(1 - x, z), core)
    remote(other, other, own_s, own_r, me, ex).wait_recv()
    hop(1, 0).start()
    hop(3, 0).start()
    share(1, 0).start()
    wsent = [remote(src, dst, w_s.at[i], w_r.at[i], sib, ex) for i, (src, dst) in enumerate(pieces(1 - core))]
    for c in wsent:
        c.start()
    wcross = remote(w_ref.at[here], w_ref.at[here], wx_s, wx_r, across, ex)
    vx[:, HD:] = jnp.ones((KB, HD), BF16)
    m_sc[...] = jnp.full_like(m_sc, -1e30)
    acc[...] = jnp.zeros_like(acc)
    for c in ql:
        c.wait()

    def block(which, start, c0, c1, masked):
        k = jnp.concatenate([kv[c0, 0], kv[c1, 0]], axis=0)
        for t in range(QROWS // TR):
            rows = pl.ds(t * TR, TR)
            s = lax.dot_general(qs[which, rows, :], k, (((1,), (1,)), ((), ())), preferred_element_type=F32)
            if masked:
                row = lax.broadcasted_iota(jnp.int32, (TR, KB), 0) % HALF + start
                lane = lax.broadcasted_iota(jnp.int32, (TR, KB), 1)
                col = lane + jnp.where(lane < CK, c0 * CK, c1 * CK - CK)
                s = jnp.where(col <= row, s, -1e30)
            old = m_sc[which, rows, :]
            new = jnp.maximum(old, jnp.max(s, axis=1, keepdims=True))
            p = jnp.exp2((s - new[:, :1]) * SCALE2)
            factor = jnp.exp2((old - new) * SCALE2)
            m_sc[which, rows, :] = new
            acc[which, rows, :] = acc[which, rows, :] * jnp.concatenate([factor, factor], axis=1) + jnp.dot(
                p.astype(BF16), vx[...], preferred_element_type=F32
            )

    @pl.loop(0, NZ)
    def _(u):
        step = jnp.where(u == NZ - 3, FAR, u)

        @pl.when(((u >= 1) & (u < FAR)) | (u == NZ - 3))
        def _():
            for flow in (0, 2, 1, 3):
                far = FAR - flow // 2

                @pl.when(step <= far)
                def _():
                    ref = piece(flow, step, core)
                    remote(ref, ref, ring_s.at[flow, step - 1], ring_r.at[flow, step - 1], me, ex).wait_recv()

                    @pl.when(step < far)
                    def _():
                        hop(flow, step).start()

                    share(flow, step).start()

        @pl.when(u == 2)
        def _():
            for i in range(NP):
                kept[i].wait()
                wsent[i].wait_recv()
            wcross.start()

        @pl.when(u == NZ - 3)
        def _():
            wcross.wait_recv()
            start_hop(w_ref, PRE, 0, snd, rcv, 0)
            start_hop(w_ref, DOWN, 0, d_s, d_r, 0)

        away = (u + 1) // 2
        odd = u % 2 == 1
        c0 = chip(jnp.where(odd | (u == 0), x, 1 - x), z - away)
        c1 = chip(jnp.where(odd & (u != NZ - 1), x, 1 - x), z + away)
        ends = (u == 0) | (u == NZ - 1)
        for flows, when in (((0, 1), ends), ((0, 2), odd & jnp.logical_not(ends)), ((1, 3), jnp.logical_not(odd | ends))):

            @pl.when(when)
            def _():
                for flow in flows:
                    shared(flow, away)

        vx[pl.ds(0, CK), :HD] = kv[c0, 1]
        vx[pl.ds(CK, CK), :HD] = kv[c1, 1]

        @pl.loop(0, 2)
        def _(which):
            start = me * TOK + which * HALF
            full = jnp.maximum(c0, c1) * CK + CK - 1 <= start
            some = jnp.minimum(c0, c1) * CK <= start

            @pl.when(full)
            def _():
                block(which, start, c0, c1, False)

            @pl.when(some & jnp.logical_not(full))
            def _():
                block(which, start, c0, c1, True)

    for which in range(2):
        for h in range(HEADS):
            rows = pl.ds(h * HALF, HALF)
            made = (acc[which, rows, :HD] / acc[which, rows, HD:]).astype(BF16)
            o_ref[pl.ds(which * HALF, HALF), pl.ds(h * HD, HD)] = made
    finish_hop(w_ref, PRE, 0, snd, rcv, 0)
    finish_hop(w_ref, DOWN, 0, d_s, d_r, 0)
    cross.wait_send()
    wcross.wait_send()
    for c in wsent:
        c.wait_send()
    for flow in range(4):
        for step in range(0 if flow < 2 else 1, FAR - flow // 2 + 1):
            share(flow, step).wait_send()
        for step in range(FAR - flow // 2):
            hop(flow, step).wait_send()


def attention(queries, keys, values, w_gate, w_up, w_down):
    dma = pltpu.SemaphoreType.DMA
    hbm = pl.BlockSpec(memory_space=HBM)
    return pl.pallas_call(
        attn_kernel,
        out_shape=(jax.ShapeDtypeStruct((TOK, HEADS * HD), BF16), WSHAPE),
        in_specs=[hbm] * 6,
        out_specs=(pl.BlockSpec(memory_space=pltpu.VMEM), hbm),
        scratch_shapes=[
            pltpu.VMEM((CHIPS, 2, CK, HD), BF16),
            pltpu.VMEM((2, QROWS, HD), BF16),
            pltpu.VMEM((2, QROWS, 2 * HD), F32),
            pltpu.VMEM((2, QROWS, HD), F32),
            pltpu.VMEM((KB, 2 * HD), BF16),
            dma((2,)), dma((2, HEADS)),
            dma, dma,
            dma((4, FAR)), dma((4, FAR)), dma((4, FAR + 1)), dma((4, FAR + 1)),
            dma((NP,)), dma((NP,)), dma((NP,)), dma, dma,
            dma((ATTN_HOPS, 2)), dma((ATTN_HOPS, 2)), dma((ATTN_DOWN, 2)), dma((ATTN_DOWN, 2)),
        ],
        compiler_params=pltpu.CompilerParams(collective_id=1, has_side_effects=True, vmem_limit_bytes=32 * MIB),
        cost_estimate=pl.CostEstimate(flops=9_000_000_000, bytes_accessed=64 * MIB, transcendentals=9_000_000),
        name="attention",
    )(*(in_hbm(a) for a in (queries, keys, values, w_gate, w_up, w_down)))


def slots(ids_ref):
    lane = lax.broadcasted_iota(jnp.int32, (ROWS, EXPERTS * CAP), 1)
    named = [ids_ref[:, k : k + 1] == lane // CAP for k in range(2)]
    has = (named[0] | named[1]).astype(F32)
    tri = lax.broadcasted_iota(jnp.int32, (ROWS, ROWS), 1) < lax.broadcasted_iota(jnp.int32, (ROWS, ROWS), 0)
    place = jnp.dot(tri.astype(F32).astype(BF16), has.astype(BF16), preferred_element_type=F32)
    here = place == (lane % CAP).astype(F32)
    return [(n & here).astype(F32) for n in named]


NB = 512
PG = 2
PC = D // PG
WL = D // NB


def project_kernel(
    o_ref, w_hbm, res_ref, gain_ref, ids_ref, e_in, arr_ref, hid_ref, e_ref,
    w, part, recv, norm, out, w_sem, rs_s, rs_r, a_s, a_r, f_s, f_r, snd, rcv, d_s, d_r,
):
    me, ex, x, z, core = place()
    sib = me + 1 - 2 * core

    def load(n):
        cols = pl.ds(pl.multiple_of(n * NB, NB), NB)
        return pltpu.make_async_copy(w_hbm.at[:, cols], w.at[n], w_sem.at[n])

    for n in range(WL):
        load(n).start()
    peers = [lax.rem(ex + d, EXP) for d in range(1, EXP)]
    greet(ring_peers() + [(sib, ex)] + [(me, p) for p in peers])
    start_hop(e_ref, PRE, ATTN_HOPS, snd, rcv, 0)
    start_hop(e_ref, DOWN, ATTN_DOWN, d_s, d_r, 0)

    def next_down(i):
        finish_hop(e_ref, DOWN, ATTN_DOWN + i, d_s, d_r, i)
        if i + 1 < PROJ_DOWN:
            start_hop(e_ref, DOWN, ATTN_DOWN + i + 1, d_s, d_r, i + 1)

    def next_hop(i):
        finish_hop(e_ref, PRE, ATTN_HOPS + i, snd, rcv, i)
        if i + 1 < PROJ_HOPS:
            start_hop(e_ref, PRE, ATTN_HOPS + i + 1, snd, rcv, i + 1)

    def share(g, d):
        p = lax.rem(ex + d, EXP)
        return remote(part.at[g, p], recv.at[g, d - 1], rs_s.at[g, d - 1], rs_r.at[g, d - 1], me, p)

    for g in range(PG):

        @pl.loop(0, PC // NB)
        def _(i):
            n = g * (PC // NB) + i
            load(n).wait()
            got = jnp.dot(o_ref[...], w[n], preferred_element_type=F32).astype(BF16)
            cols = pl.ds(pl.multiple_of(i * NB, NB), NB)
            for b in range(EXP):
                part[g, b, :, cols] = got[b * ROWS : (b + 1) * ROWS, :]

        for d in range(1, EXP):
            share(g, d).start()

    next_hop(0)
    for g in range(PG):
        if g == 0:
            next_hop(1)
            next_down(0)
        for d in range(1, EXP):
            share(g, d).wait_recv()

        @pl.loop(0, PC // NB)
        def _(i):
            cols = pl.ds(pl.multiple_of(i * NB, NB), NB)
            total = part[g, ex, :, cols].astype(F32)
            for d in range(EXP - 1):
                total += recv[g, d, :, cols].astype(F32)
            full = pl.ds(pl.multiple_of(g * PC + i * NB, NB), NB)
            hid_ref[:, full] = (res_ref[:, full].astype(F32) + total).astype(BF16)

    state = hid_ref[...].astype(F32)
    inv = 1.0 / jnp.sqrt(jnp.mean(state * state, axis=1, keepdims=True) + 1e-06)
    norm[...] = (state * inv * gain_ref[...].astype(F32)).astype(BF16)
    first, second = slots(ids_ref)
    table = (first + second).T.astype(BF16)
    out[...] = jnp.dot(table, norm[...], preferred_element_type=F32).astype(BF16).reshape(EXPERTS, CAP, D)

    def give_rows(d):
        p = lax.rem(ex + d, EXP)
        return remote(out.at[p], arr_ref.at[0, ex], a_s.at[d - 1], a_r.at[d - 1], me, p)

    def forward(d):
        source = lax.rem(ex + EXP - d, EXP)
        return remote(arr_ref.at[0, source], arr_ref.at[1, source], f_s.at[d], f_r.at[d], sib, ex)

    for d in range(1, EXP):
        give_rows(d).start()
    arr_ref[0, ex] = out[ex]
    forward(0).start()
    next_hop(2)
    for d in range(1, EXP):
        if d == EXP // 2:
            next_hop(3)
            next_down(1)
        source = lax.rem(ex + EXP - d, EXP)
        remote(out.at[ex], arr_ref.at[0, source], a_s.at[d - 1], a_r.at[d - 1], me, ex).wait_recv()
        forward(d).start()
    for d in range(EXP):
        forward(d).wait()
    next_hop(4)
    for d in range(1, EXP):
        for g in range(PG):
            share(g, d).wait_send()
        give_rows(d).wait_send()


def project(attn, w_out, residual, gain, ids, weights):
    dma = pltpu.SemaphoreType.DMA
    vmem, hbm = pl.BlockSpec(memory_space=pltpu.VMEM), pl.BlockSpec(memory_space=HBM)
    return pl.pallas_call(
        project_kernel,
        out_shape=(
            jax.ShapeDtypeStruct((NC, EXPERTS, CAP, D), BF16),
            jax.ShapeDtypeStruct((ROWS, D), BF16),
            WSHAPE,
        ),
        in_specs=[vmem, hbm, vmem, vmem, vmem, hbm],
        out_specs=(vmem, vmem, hbm),
        input_output_aliases={5: 2},
        scratch_shapes=[
            pltpu.VMEM((WL, HEADS * HD, NB), BF16),
            pltpu.VMEM((PG, EXP, ROWS, PC), BF16),
            pltpu.VMEM((PG, EXP - 1, ROWS, PC), BF16),
            pltpu.VMEM((ROWS, D), BF16),
            pltpu.VMEM((EXPERTS, CAP, D), BF16),
            dma((WL,)), dma((PG, EXP - 1)), dma((PG, EXP - 1)), dma((EXP - 1,)), dma((EXP - 1,)),
            dma((EXP,)), dma((EXP,)), dma((PROJ_HOPS, 2)), dma((PROJ_HOPS, 2)),
            dma((PROJ_DOWN, 2)), dma((PROJ_DOWN, 2)),
        ],
        compiler_params=pltpu.CompilerParams(collective_id=2, has_side_effects=True, vmem_limit_bytes=40 * MIB),
        cost_estimate=pl.CostEstimate(flops=2_200_000_000, bytes_accessed=64 * MIB, transcendentals=0),
        name="project_dispatch",
    )(attn, in_hbm(w_out), residual, gain, ids, in_hbm(weights))


SLOTS = EXPERTS * CAP
DEPTH = NC * 128
GCOLS = NC * DEPTH


def expert_kernel(
    arr_ref, w_in, hid_ref, ids_ref, gates_ref, o_ref, w_hbm,
    w, pre, act, mine, theirs, other, res, got, p_sem, d_sem, x_s, x_r, r_s, r_r, snd, rcv, d_s, d_r,
):
    me, ex, x, z, core = place()
    sib = me + 1 - 2 * core
    held = ATTN_HOPS + PROJ_HOPS + 1

    def at(step, way):
        return chip(x, z - step) if way == 0 else chip(1 - x, z + step)

    def load(kind, sem, step, way):
        c = at(step, way)
        return pltpu.make_async_copy(w_hbm.at[c, :, kind], w.at[c, :, kind], sem.at[step, way])

    for step in range(held):
        for way in range(2):
            load(PRE, p_sem, step, way).start()
    for step in range(DOWN_HELD):
        for way in range(2):
            load(DOWN, d_sem, step, way).start()
    peers = [lax.rem(ex + d, EXP) for d in range(1, EXP)]
    greet(ring_peers() + [(sib, ex)] + [(me, p) for p in peers])
    start_hop(w_hbm, PRE, held - 1, snd, rcv, 0)
    start_hop(w_hbm, DOWN, DOWN_HELD - 1, d_s, d_r, 0)
    pre[...] = jnp.zeros_like(pre)

    def use(step):
        for way in range(2):
            load(PRE, p_sem, step, way).wait()
            j = at(step, way)
            cols = pl.ds(pl.multiple_of(j * DEPTH, DEPTH), DEPTH)
            rows = arr_ref[:, :, :, cols].reshape(NC * SLOTS, DEPTH)
            tiles = [
                jnp.concatenate([w[j, c, pl.ds(t * 128, 128)] for c in range(NC)], axis=0) for t in range(2 * TILES)
            ]
            pre[...] += jnp.dot(rows, jnp.concatenate(tiles, axis=1), preferred_element_type=F32)

    def next_down(i):
        slot = i - DOWN_HELD + 1
        finish_hop(w_hbm, DOWN, i, d_s, d_r, slot)
        if i + 1 < NZ - 1:
            start_hop(w_hbm, DOWN, i + 1, d_s, d_r, slot + 1)
        for way in range(2):
            load(DOWN, d_sem, i + 1, way).start()

    @pl.loop(0, held)
    def _(step):
        use(step)

    next_down(DOWN_HELD - 1)
    for i in range(EXPERT_HOPS):
        finish_hop(w_hbm, PRE, held - 1 + i, snd, rcv, i)
        if i + 1 < EXPERT_HOPS:
            start_hop(w_hbm, PRE, held + i, snd, rcv, i + 1)
        for way in range(2):
            load(PRE, p_sem, held + i, way).start()
        use(held + i)

    gate = pre[:, :FH]
    act[...] = (gate / (1.0 + jnp.exp(-gate)) * pre[:, FH:]).astype(BF16)

    def swap(t):
        return remote(theirs.at[t], other.at[t], x_s.at[t], x_r.at[t], sib, ex)

    def give(t, d):
        p = lax.rem(ex + d, EXP)
        return remote(res.at[t, p], got.at[t, ex], r_s.at[t, d - 1], r_r.at[t, d - 1], me, p)

    def finish(t):
        swap(t).wait_recv()
        res[t] = (mine[t] + other[t]).astype(BF16).reshape(EXPERTS, CAP, GCOLS)
        for d in range(1, EXP):
            give(t, d).start()
        got[t, ex] = res[t, ex]

    first, second = slots(ids_ref)
    picks = jnp.concatenate([first, second], axis=0).astype(BF16)
    weight = [gates_ref[:, k : k + 1] for k in range(2)]

    def combine(t):
        for d in range(1, EXP):
            source = lax.rem(ex + EXP - d, EXP)
            remote(res.at[t, ex], got.at[t, source], r_s.at[t, d - 1], r_r.at[t, d - 1], me, ex).wait_recv()
        both = jnp.dot(picks, got[t].reshape(SLOTS, GCOLS), preferred_element_type=F32)
        total = weight[0] * both[:ROWS] + weight[1] * both[ROWS:]
        for way in range(2):
            cols = pl.ds(pl.multiple_of(at(t, way) * DEPTH, DEPTH), DEPTH)
            part = total[:, way * DEPTH : (way + 1) * DEPTH]
            o_ref[:, cols] = (hid_ref[:, cols].astype(F32) + part).astype(BF16)

    for t in range(NZ):
        if t in TAKEN:
            next_down(DOWN_HELD + TAKEN.index(t))
        for way in range(2):
            load(DOWN, d_sem, t, way).wait()
            down = jnp.concatenate([w[at(t, way), c, DOWN] for c in range(NC)], axis=1)
            made = jnp.dot(act[...], down, preferred_element_type=F32)
            mine[t, :, way * DEPTH : (way + 1) * DEPTH] = made[:SLOTS]
            theirs[t, :, way * DEPTH : (way + 1) * DEPTH] = made[SLOTS:]
        swap(t).start()
        if t >= 1:
            finish(t - 1)
        if t >= LAG:
            combine(t - LAG)
    finish(NZ - 1)
    for t in range(NZ - LAG, NZ):
        combine(t)
    for t in range(NZ):
        swap(t).wait_send()
        for d in range(1, EXP):
            give(t, d).wait_send()


LAG = 4
TAKEN = (1, 3, 6)


def experts(arrived, weights, hidden, ids, gates):
    vmem, hbm = pl.BlockSpec(memory_space=pltpu.VMEM), pl.BlockSpec(memory_space=HBM)
    return pl.pallas_call(
        expert_kernel,
        out_shape=(jax.ShapeDtypeStruct((ROWS, D), BF16), WSHAPE),
        in_specs=[vmem, hbm, vmem, vmem, vmem],
        out_specs=(vmem, hbm),
        input_output_aliases={1: 1},
        scratch_shapes=[
            pltpu.VMEM((CHIPS, NC, 3 * FH, 128), BF16),
            pltpu.VMEM((NC * SLOTS, 2 * FH), F32),
            pltpu.VMEM((NC * SLOTS, FH), BF16),
            pltpu.VMEM((NZ, SLOTS, GCOLS), F32),
            pltpu.VMEM((NZ, SLOTS, GCOLS), F32),
            pltpu.VMEM((NZ, SLOTS, GCOLS), F32),
            pltpu.VMEM((NZ, EXPERTS, CAP, GCOLS), BF16),
            pltpu.VMEM((NZ, EXPERTS, CAP, GCOLS), BF16),
            pltpu.SemaphoreType.DMA((NZ, 2)),
            pltpu.SemaphoreType.DMA((NZ, 2)),
            pltpu.SemaphoreType.DMA((NZ,)),
            pltpu.SemaphoreType.DMA((NZ,)),
            pltpu.SemaphoreType.DMA((NZ, EXP - 1)),
            pltpu.SemaphoreType.DMA((NZ, EXP - 1)),
            pltpu.SemaphoreType.DMA((EXPERT_HOPS, 2)),
            pltpu.SemaphoreType.DMA((EXPERT_HOPS, 2)),
            pltpu.SemaphoreType.DMA((NZ - DOWN_HELD, 2)),
            pltpu.SemaphoreType.DMA((NZ - DOWN_HELD, 2)),
        ],
        compiler_params=pltpu.CompilerParams(collective_id=3, has_side_effects=True, vmem_limit_bytes=48 * MIB),
        cost_estimate=pl.CostEstimate(flops=2_500_000_000, bytes_accessed=32 * MIB, transcendentals=100_000),
        name="experts",
    )(arrived, in_hbm(weights), hidden, ids, gates)[0]


def body(queries, keys, values, w_out, residual, norm_gain, expert_ids, gate_weights, w_gate, w_up, w_down):
    attn, weights = attention(queries, keys, values, w_gate[0], w_up[0], w_down[0])
    arrived, hidden, weights = project(attn, w_out, residual, norm_gain.reshape(1, D), expert_ids, weights)
    return experts(arrived, weights, hidden, expert_ids, gate_weights)


def solution(mesh):
    placed = (
        P("ctx", "exp"),
        P("ctx", None),
        P("ctx", None),
        P("exp", None),
        P(("ctx", "exp"), None),
        P(),
        P(("ctx", "exp"), None),
        P(("ctx", "exp"), None),
        P("exp", "ctx", None),
        P("exp", "ctx", None),
        P("exp", None, "ctx"),
    )
    return jax.shard_map(
        body, mesh=mesh, in_specs=placed, out_specs=P(("ctx", "exp"), None), check_vma=False
    )
```

```python
import functools
import math

import jax
import jax.numpy as jnp
from jax import lax
from jax.experimental import pallas as pl
from jax.experimental.pallas import tpu as pltpu
from jax.sharding import PartitionSpec as P

D = 4096
HQ = 64
KVH = 4
HD = 128
FF = 768
EXPERTS = 8
CAP = 16
ROWS = 32
NX, NZ, NC = 2, 8, 2
CTX = NX * NZ * NC
EXP = 8
TOK = 256
HALF = 128
HEADS = HQ // EXP
MESH = pl.DeviceIdType.MESH
MIB = 1 << 20
F32 = jnp.float32
BF16 = jnp.bfloat16


def remote(src, dst, send, recv, ctx, exp):
    return pltpu.make_async_remote_copy(
        src_ref=src, dst_ref=dst, send_sem=send, recv_sem=recv, device_id=(ctx, exp), device_id_type=MESH
    )


def greet(peers):
    barrier = pltpu.get_barrier_semaphore()
    for ctx, exp in peers:
        pl.semaphore_signal(barrier, inc=1, device_id=(ctx, exp), device_id_type=MESH)
    pl.semaphore_wait(barrier, len(peers))


def place():
    me = lax.axis_index("ctx")
    return me, lax.axis_index("exp"), me // (NZ * NC), (me // NC) % NZ, me % NC


def chunk(x, z, core):
    return x * (NZ * NC) + lax.rem(z + 2 * NZ, NZ) * NC + core


def chip(x, z):
    return x * NZ + lax.rem(z + 2 * NZ, NZ)


def hop_copies(w_ref, kind, hop, snd, rcv, slot):
    me, ex, x, z, core = place()
    out = []
    for way, (xx, step) in enumerate(((x, 1), (1 - x, -1))):
        ref = w_ref.at[chip(xx, z - step * hop), :, kind]
        out.append(remote(ref, ref, snd.at[slot, way], rcv.at[slot, way], chunk(x, z + step, core), ex))
    return out


def start_hop(*a):
    for c in hop_copies(*a):
        c.start()


def finish_hop(w_ref, kind, hop, snd, rcv, slot):
    me, ex, x, z, core = place()
    for way, (xx, step) in enumerate(((x, 1), (1 - x, -1))):
        ref = w_ref.at[chip(xx, z - step * (hop + 1)), :, kind]
        remote(ref, ref, snd.at[slot, way], rcv.at[slot, way], me, ex).wait_recv()
    for c in hop_copies(w_ref, kind, hop, snd, rcv, slot):
        c.wait_send()


def ring_peers():
    me, ex, x, z, core = place()
    return [(chunk(x, z + 1, core), ex), (chunk(x, z - 1, core), ex)]


HBM = pltpu.HBM
TILES = FF // NC // 128
FH = FF // NC
CHIPS = CTX // NC
WSHAPE = HBM((CHIPS, NC, 3 * FH, 128), BF16)


def in_hbm(x):
    return pltpu.with_memory_space_constraint(x, HBM)


PRE, DOWN = pl.ds(0, 2 * FH), pl.ds(2 * FH, FH)
ATTN_HOPS, PROJ_HOPS = 2, 5
ATTN_DOWN, PROJ_DOWN = 1, 2
DOWN_HELD = ATTN_DOWN + PROJ_DOWN + 1


CK = NC * TOK
KB = 2 * CK
TR = 128
QROWS = HEADS * HALF
SCALE2 = math.log2(math.e) / math.sqrt(HD)
NP = 2 * TILES + 1
FAR = NZ // 2


def attn_kernel(
    q_ref, k_ref, v_ref, g_ref, u_ref, d_ref, o_ref, w_ref,
    kv, qs, acc, m_sc, vx,
    kv_l, q_l, own_s, own_r, ring_s, ring_r, sib_s, sib_r, w_l, w_s, w_r, wx_s, wx_r, snd, rcv, d_s, d_r,
):
    me, ex, x, z, core = place()
    up, down = chunk(x, z + 1, core), chunk(x, z - 1, core)
    across, sib = chunk(1 - x, z, core), chunk(x, z, 1 - core)
    here = chip(x, z)
    head = pl.ds(pl.multiple_of((ex // 2) * HD, HD), HD)

    def part(c, cc):
        return kv.at[c, :, pl.ds(pl.multiple_of(cc * TOK, TOK), TOK)]

    def pieces(half):
        for a, ref in enumerate((g_ref, u_ref)):
            for t in range(TILES):
                cols = pl.ds(pl.multiple_of(half * FH + t * 128, 128), 128)
                yield ref.at[:, cols], w_ref.at[here, core, pl.ds((a * TILES + t) * 128, 128)]
        yield d_ref.at[pl.ds(pl.multiple_of(half * FH, FH), FH)], w_ref.at[here, core, pl.ds(2 * FH, FH)]

    rows0 = pl.ds(pl.multiple_of(core * TOK, TOK), TOK)
    kvl = [
        pltpu.make_async_copy(ref.at[:, head], kv.at[here, i, rows0], kv_l.at[i]) for i, ref in enumerate((k_ref, v_ref))
    ]
    ql = [
        pltpu.make_async_copy(
            q_ref.at[pl.ds(a * HALF, HALF), pl.ds(h * HD, HD)], qs.at[a, pl.ds(h * HALF, HALF)], q_l.at[a, h]
        )
        for a in range(2)
        for h in range(HEADS)
    ]
    kept = [pltpu.make_async_copy(src, dst, w_l.at[i]) for i, (src, dst) in enumerate(pieces(core))]
    for c in kvl + ql + kept:
        c.start()
    greet([(up, ex), (down, ex), (across, ex), (sib, ex)])
    for c in kvl:
        c.wait()

    def piece(flow, step, cc):
        return part(chip(x if flow in (0, 2) else 1 - x, z - step if flow in (0, 3) else z + step), cc)

    def hop(flow, step):
        ref = piece(flow, step, core)
        target = up if flow in (0, 3) else down
        return remote(ref, ref, ring_s.at[flow, step], ring_r.at[flow, step], target, ex)

    def share(flow, step):
        ref = piece(flow, step, core)
        return remote(ref, ref, sib_s.at[flow, step], sib_r.at[flow, step], sib, ex)

    def shared(way, step):
        ref = piece(way, step, 1 - core)
        remote(ref, ref, sib_s.at[way, step], sib_r.at[way, step], me, ex).wait_recv()

    own = part(here, core)
    cross = remote(own, own, own_s, own_r, across, ex)
    cross.start()
    hop(0, 0).start()
    hop(2, 0).start()
    share(0, 0).start()
    other = part(chip(1 - x, z), core)
    remote(other, other, own_s, own_r, me, ex).wait_recv()
    hop(1, 0).start()
    hop(3, 0).start()
    share(1, 0).start()
    wsent = [remote(src, dst, w_s.at[i], w_r.at[i], sib, ex) for i, (src, dst) in enumerate(pieces(1 - core))]
    for c in wsent:
        c.start()
    wcross = remote(w_ref.at[here], w_ref.at[here], wx_s, wx_r, across, ex)
    vx[:, HD:] = jnp.ones((KB, HD), BF16)
    m_sc[...] = jnp.full_like(m_sc, -1e30)
    acc[...] = jnp.zeros_like(acc)
    for c in ql:
        c.wait()

    def block(which, start, c0, c1, masked):
        k = jnp.concatenate([kv[c0, 0], kv[c1, 0]], axis=0)
        for t in range(QROWS // TR):
            rows = pl.ds(t * TR, TR)
            s = lax.dot_general(qs[which, rows, :], k, (((1,), (1,)), ((), ())), preferred_element_type=F32)
            if masked:
                row = lax.broadcasted_iota(jnp.int32, (TR, KB), 0) % HALF + start
                lane = lax.broadcasted_iota(jnp.int32, (TR, KB), 1)
                col = lane + jnp.where(lane < CK, c0 * CK, c1 * CK - CK)
                s = jnp.where(col <= row, s, -1e30)
            old = m_sc[which, rows, :]
            new = jnp.maximum(old, jnp.max(s, axis=1, keepdims=True))
            p = jnp.exp2((s - new[:, :1]) * SCALE2)
            factor = jnp.exp2((old - new) * SCALE2)
            m_sc[which, rows, :] = new
            acc[which, rows, :] = acc[which, rows, :] * jnp.concatenate([factor, factor], axis=1) + jnp.dot(
                p.astype(BF16), vx[...], preferred_element_type=F32
            )

    @pl.loop(0, NZ)
    def _(u):
        step = jnp.where(u == NZ - 3, FAR, u)

        @pl.when(((u >= 1) & (u < FAR)) | (u == NZ - 3))
        def _():
            for flow in (0, 2, 1, 3):
                far = FAR - flow // 2

                @pl.when(step <= far)
                def _():
                    ref = piece(flow, step, core)
                    remote(ref, ref, ring_s.at[flow, step - 1], ring_r.at[flow, step - 1], me, ex).wait_recv()

                    @pl.when(step < far)
                    def _():
                        hop(flow, step).start()

                    share(flow, step).start()

        @pl.when(u == 1)
        def _():
            for i in range(NP):
                kept[i].wait()
                wsent[i].wait_recv()
            wcross.start()

        @pl.when(u == FAR)
        def _():
            wcross.wait_recv()
            start_hop(w_ref, PRE, 0, snd, rcv, 0)
            start_hop(w_ref, DOWN, 0, d_s, d_r, 0)

        @pl.when(u == NZ - 1)
        def _():
            finish_hop(w_ref, PRE, 0, snd, rcv, 0)
            start_hop(w_ref, PRE, 1, snd, rcv, 1)

        away = (u + 1) // 2
        odd = u % 2 == 1
        c0 = chip(jnp.where(odd | (u == 0), x, 1 - x), z - away)
        c1 = chip(jnp.where(odd & (u != NZ - 1), x, 1 - x), z + away)
        ends = (u == 0) | (u == NZ - 1)
        for flows, when in (((0, 1), ends), ((0, 2), odd & jnp.logical_not(ends)), ((1, 3), jnp.logical_not(odd | ends))):

            @pl.when(when)
            def _():
                for flow in flows:
                    shared(flow, away)

        vx[pl.ds(0, CK), :HD] = kv[c0, 1]
        vx[pl.ds(CK, CK), :HD] = kv[c1, 1]

        @pl.loop(0, 2)
        def _(which):
            start = me * TOK + which * HALF
            full = jnp.maximum(c0, c1) * CK + CK - 1 <= start
            some = jnp.minimum(c0, c1) * CK <= start

            @pl.when(full)
            def _():
                block(which, start, c0, c1, False)

            @pl.when(some & jnp.logical_not(full))
            def _():
                block(which, start, c0, c1, True)

    for which in range(2):
        for h in range(HEADS):
            rows = pl.ds(h * HALF, HALF)
            made = (acc[which, rows, :HD] / acc[which, rows, HD:]).astype(BF16)
            o_ref[pl.ds(which * HALF, HALF), pl.ds(h * HD, HD)] = made
    finish_hop(w_ref, PRE, 1, snd, rcv, 1)
    finish_hop(w_ref, DOWN, 0, d_s, d_r, 0)
    cross.wait_send()
    wcross.wait_send()
    for c in wsent:
        c.wait_send()
    for flow in range(4):
        for step in range(0 if flow < 2 else 1, FAR - flow // 2 + 1):
            share(flow, step).wait_send()
        for step in range(FAR - flow // 2):
            hop(flow, step).wait_send()


def attention(queries, keys, values, w_gate, w_up, w_down):
    dma = pltpu.SemaphoreType.DMA
    hbm = pl.BlockSpec(memory_space=HBM)
    return pl.pallas_call(
        attn_kernel,
        out_shape=(jax.ShapeDtypeStruct((TOK, HEADS * HD), BF16), WSHAPE),
        in_specs=[hbm] * 6,
        out_specs=(pl.BlockSpec(memory_space=pltpu.VMEM), hbm),
        scratch_shapes=[
            pltpu.VMEM((CHIPS, 2, CK, HD), BF16),
            pltpu.VMEM((2, QROWS, HD), BF16),
            pltpu.VMEM((2, QROWS, 2 * HD), F32),
            pltpu.VMEM((2, QROWS, HD), F32),
            pltpu.VMEM((KB, 2 * HD), BF16),
            dma((2,)), dma((2, HEADS)),
            dma, dma,
            dma((4, FAR)), dma((4, FAR)), dma((4, FAR + 1)), dma((4, FAR + 1)),
            dma((NP,)), dma((NP,)), dma((NP,)), dma, dma,
            dma((ATTN_HOPS, 2)), dma((ATTN_HOPS, 2)), dma((ATTN_DOWN, 2)), dma((ATTN_DOWN, 2)),
        ],
        compiler_params=pltpu.CompilerParams(collective_id=1, has_side_effects=True, vmem_limit_bytes=32 * MIB),
        cost_estimate=pl.CostEstimate(flops=9_000_000_000, bytes_accessed=64 * MIB, transcendentals=9_000_000),
        name="attention",
    )(*(in_hbm(a) for a in (queries, keys, values, w_gate, w_up, w_down)))


def slots(ids_ref):
    lane = lax.broadcasted_iota(jnp.int32, (ROWS, EXPERTS * CAP), 1)
    named = [ids_ref[:, k : k + 1] == lane // CAP for k in range(2)]
    has = (named[0] | named[1]).astype(F32)
    tri = lax.broadcasted_iota(jnp.int32, (ROWS, ROWS), 1) < lax.broadcasted_iota(jnp.int32, (ROWS, ROWS), 0)
    place = jnp.dot(tri.astype(F32).astype(BF16), has.astype(BF16), preferred_element_type=F32)
    here = place == (lane % CAP).astype(F32)
    return [(n & here).astype(F32) for n in named]


NB = 512
PG = 2
PC = D // PG
WL = D // NB


def project_kernel(
    o_ref, w_hbm, res_ref, gain_ref, ids_ref, e_in, arr_ref, hid_ref, e_ref,
    w, part, recv, norm, out, w_sem, rs_s, rs_r, a_s, a_r, f_s, f_r, snd, rcv, d_s, d_r,
):
    me, ex, x, z, core = place()
    sib = me + 1 - 2 * core

    def load(n):
        cols = pl.ds(pl.multiple_of(n * NB, NB), NB)
        return pltpu.make_async_copy(w_hbm.at[:, cols], w.at[n], w_sem.at[n])

    for n in range(WL):
        load(n).start()
    peers = [lax.rem(ex + d, EXP) for d in range(1, EXP)]
    greet(ring_peers() + [(sib, ex)] + [(me, p) for p in peers])
    start_hop(e_ref, PRE, ATTN_HOPS, snd, rcv, 0)
    start_hop(e_ref, DOWN, ATTN_DOWN, d_s, d_r, 0)

    def next_down(i):
        finish_hop(e_ref, DOWN, ATTN_DOWN + i, d_s, d_r, i)
        if i + 1 < PROJ_DOWN:
            start_hop(e_ref, DOWN, ATTN_DOWN + i + 1, d_s, d_r, i + 1)

    def next_hop(i):
        finish_hop(e_ref, PRE, ATTN_HOPS + i, snd, rcv, i)
        if i + 1 < PROJ_HOPS:
            start_hop(e_ref, PRE, ATTN_HOPS + i + 1, snd, rcv, i + 1)

    def share(g, d):
        p = lax.rem(ex + d, EXP)
        return remote(part.at[g, p], recv.at[g, d - 1], rs_s.at[g, d - 1], rs_r.at[g, d - 1], me, p)

    for g in range(PG):

        @pl.loop(0, PC // NB)
        def _(i):
            n = g * (PC // NB) + i
            load(n).wait()
            got = jnp.dot(o_ref[...], w[n], preferred_element_type=F32).astype(BF16)
            cols = pl.ds(pl.multiple_of(i * NB, NB), NB)
            for b in range(EXP):
                part[g, b, :, cols] = got[b * ROWS : (b + 1) * ROWS, :]

        for d in range(1, EXP):
            share(g, d).start()

    next_hop(0)
    for g in range(PG):
        if g == 0:
            next_hop(1)
            next_down(0)
        for d in range(1, EXP):
            share(g, d).wait_recv()

        @pl.loop(0, PC // NB)
        def _(i):
            cols = pl.ds(pl.multiple_of(i * NB, NB), NB)
            total = part[g, ex, :, cols].astype(F32)
            for d in range(EXP - 1):
                total += recv[g, d, :, cols].astype(F32)
            full = pl.ds(pl.multiple_of(g * PC + i * NB, NB), NB)
            hid_ref[:, full] = (res_ref[:, full].astype(F32) + total).astype(BF16)

    state = hid_ref[...].astype(F32)
    inv = 1.0 / jnp.sqrt(jnp.mean(state * state, axis=1, keepdims=True) + 1e-06)
    norm[...] = (state * inv * gain_ref[...].astype(F32)).astype(BF16)
    first, second = slots(ids_ref)
    table = (first + second).T.astype(BF16)
    out[...] = jnp.dot(table, norm[...], preferred_element_type=F32).astype(BF16).reshape(EXPERTS, CAP, D)

    def give_rows(d):
        p = lax.rem(ex + d, EXP)
        return remote(out.at[p], arr_ref.at[0, ex], a_s.at[d - 1], a_r.at[d - 1], me, p)

    def forward(d):
        source = lax.rem(ex + EXP - d, EXP)
        return remote(arr_ref.at[0, source], arr_ref.at[1, source], f_s.at[d], f_r.at[d], sib, ex)

    for d in range(1, EXP):
        give_rows(d).start()
    arr_ref[0, ex] = out[ex]
    forward(0).start()
    next_hop(2)
    for d in range(1, EXP):
        if d == EXP // 2:
            next_hop(3)
            next_down(1)
        source = lax.rem(ex + EXP - d, EXP)
        remote(out.at[ex], arr_ref.at[0, source], a_s.at[d - 1], a_r.at[d - 1], me, ex).wait_recv()
        forward(d).start()
    for d in range(EXP):
        forward(d).wait()
    next_hop(4)
    for d in range(1, EXP):
        for g in range(PG):
            share(g, d).wait_send()
        give_rows(d).wait_send()


def project(attn, w_out, residual, gain, ids, weights):
    dma = pltpu.SemaphoreType.DMA
    vmem, hbm = pl.BlockSpec(memory_space=pltpu.VMEM), pl.BlockSpec(memory_space=HBM)
    return pl.pallas_call(
        project_kernel,
        out_shape=(
            jax.ShapeDtypeStruct((NC, EXPERTS, CAP, D), BF16),
            jax.ShapeDtypeStruct((ROWS, D), BF16),
            WSHAPE,
        ),
        in_specs=[vmem, hbm, vmem, vmem, vmem, hbm],
        out_specs=(vmem, vmem, hbm),
        input_output_aliases={5: 2},
        scratch_shapes=[
            pltpu.VMEM((WL, HEADS * HD, NB), BF16),
            pltpu.VMEM((PG, EXP, ROWS, PC), BF16),
            pltpu.VMEM((PG, EXP - 1, ROWS, PC), BF16),
            pltpu.VMEM((ROWS, D), BF16),
            pltpu.VMEM((EXPERTS, CAP, D), BF16),
            dma((WL,)), dma((PG, EXP - 1)), dma((PG, EXP - 1)), dma((EXP - 1,)), dma((EXP - 1,)),
            dma((EXP,)), dma((EXP,)), dma((PROJ_HOPS, 2)), dma((PROJ_HOPS, 2)),
            dma((PROJ_DOWN, 2)), dma((PROJ_DOWN, 2)),
        ],
        compiler_params=pltpu.CompilerParams(collective_id=2, has_side_effects=True, vmem_limit_bytes=40 * MIB),
        cost_estimate=pl.CostEstimate(flops=2_200_000_000, bytes_accessed=64 * MIB, transcendentals=0),
        name="project_dispatch",
    )(attn, in_hbm(w_out), residual, gain, ids, in_hbm(weights))


SLOTS = EXPERTS * CAP
DEPTH = NC * 128
GCOLS = NC * DEPTH


def expert_kernel(
    arr_ref, w_in, hid_ref, ids_ref, gates_ref, o_ref, w_hbm,
    w, pre, act, mine, theirs, other, res, got, p_sem, d_sem, x_s, x_r, r_s, r_r, d_s, d_r,
):
    me, ex, x, z, core = place()
    sib = me + 1 - 2 * core

    def at(step, way):
        return chip(x, z - step) if way == 0 else chip(1 - x, z + step)

    def load(kind, sem, step, way):
        c = at(step, way)
        return pltpu.make_async_copy(w_hbm.at[c, :, kind], w.at[c, :, kind], sem.at[step, way])

    for step in range(NZ):
        for way in range(2):
            load(PRE, p_sem, step, way).start()
    for step in range(DOWN_HELD):
        for way in range(2):
            load(DOWN, d_sem, step, way).start()
    peers = [lax.rem(ex + d, EXP) for d in range(1, EXP)]
    greet(ring_peers() + [(sib, ex)] + [(me, p) for p in peers])
    start_hop(w_hbm, DOWN, DOWN_HELD - 1, d_s, d_r, 0)
    pre[...] = jnp.zeros_like(pre)

    def use(step):
        for way in range(2):
            load(PRE, p_sem, step, way).wait()
            j = at(step, way)
            cols = pl.ds(pl.multiple_of(j * DEPTH, DEPTH), DEPTH)
            rows = arr_ref[:, :, :, cols].reshape(NC * SLOTS, DEPTH)
            tiles = [
                jnp.concatenate([w[j, c, pl.ds(t * 128, 128)] for c in range(NC)], axis=0) for t in range(2 * TILES)
            ]
            pre[...] += jnp.dot(rows, jnp.concatenate(tiles, axis=1), preferred_element_type=F32)

    def next_down(i):
        slot = i - DOWN_HELD + 1
        finish_hop(w_hbm, DOWN, i, d_s, d_r, slot)
        if i + 1 < NZ - 1:
            start_hop(w_hbm, DOWN, i + 1, d_s, d_r, slot + 1)
        for way in range(2):
            load(DOWN, d_sem, i + 1, way).start()

    for half in range(2):

        @pl.loop(half * NZ // 2, (half + 1) * NZ // 2)
        def _(step):
            use(step)

        next_down(DOWN_HELD - 1 + half)

    gate = pre[:, :FH]
    act[...] = (gate / (1.0 + jnp.exp(-gate)) * pre[:, FH:]).astype(BF16)

    def swap(t):
        return remote(theirs.at[t], other.at[t], x_s.at[t], x_r.at[t], sib, ex)

    def give(t, d):
        p = lax.rem(ex + d, EXP)
        return remote(res.at[t, p], got.at[t, ex], r_s.at[t, d - 1], r_r.at[t, d - 1], me, p)

    def finish(t):
        swap(t).wait_recv()
        res[t] = (mine[t] + other[t]).astype(BF16).reshape(EXPERTS, CAP, GCOLS)
        for d in range(1, EXP):
            give(t, d).start()
        got[t, ex] = res[t, ex]

    first, second = slots(ids_ref)
    picks = jnp.concatenate([first, second], axis=0).astype(BF16)
    weight = [gates_ref[:, k : k + 1] for k in range(2)]

    def combine(t):
        for d in range(1, EXP):
            source = lax.rem(ex + EXP - d, EXP)
            remote(res.at[t, ex], got.at[t, source], r_s.at[t, d - 1], r_r.at[t, d - 1], me, ex).wait_recv()
        both = jnp.dot(picks, got[t].reshape(SLOTS, GCOLS), preferred_element_type=F32)
        total = weight[0] * both[:ROWS] + weight[1] * both[ROWS:]
        for way in range(2):
            cols = pl.ds(pl.multiple_of(at(t, way) * DEPTH, DEPTH), DEPTH)
            part = total[:, way * DEPTH : (way + 1) * DEPTH]
            o_ref[:, cols] = (hid_ref[:, cols].astype(F32) + part).astype(BF16)

    for t in range(NZ):
        if t in TAKEN:
            next_down(DOWN_HELD + 1 + TAKEN.index(t))
        for way in range(2):
            load(DOWN, d_sem, t, way).wait()
            down = jnp.concatenate([w[at(t, way), c, DOWN] for c in range(NC)], axis=1)
            made = jnp.dot(act[...], down, preferred_element_type=F32)
            mine[t, :, way * DEPTH : (way + 1) * DEPTH] = made[:SLOTS]
            theirs[t, :, way * DEPTH : (way + 1) * DEPTH] = made[SLOTS:]
        swap(t).start()
        if t >= 1:
            finish(t - 1)
        if t >= LAG:
            combine(t - LAG)
    finish(NZ - 1)
    for t in range(NZ - LAG, NZ):
        combine(t)
    for t in range(NZ):
        swap(t).wait_send()
        for d in range(1, EXP):
            give(t, d).wait_send()


LAG = 4
TAKEN = (2, 5)


def experts(arrived, weights, hidden, ids, gates):
    vmem, hbm = pl.BlockSpec(memory_space=pltpu.VMEM), pl.BlockSpec(memory_space=HBM)
    return pl.pallas_call(
        expert_kernel,
        out_shape=(jax.ShapeDtypeStruct((ROWS, D), BF16), WSHAPE),
        in_specs=[vmem, hbm, vmem, vmem, vmem],
        out_specs=(vmem, hbm),
        input_output_aliases={1: 1},
        scratch_shapes=[
            pltpu.VMEM((CHIPS, NC, 3 * FH, 128), BF16),
            pltpu.VMEM((NC * SLOTS, 2 * FH), F32),
            pltpu.VMEM((NC * SLOTS, FH), BF16),
            pltpu.VMEM((NZ, SLOTS, GCOLS), F32),
            pltpu.VMEM((NZ, SLOTS, GCOLS), F32),
            pltpu.VMEM((NZ, SLOTS, GCOLS), F32),
            pltpu.VMEM((NZ, EXPERTS, CAP, GCOLS), BF16),
            pltpu.VMEM((NZ, EXPERTS, CAP, GCOLS), BF16),
            pltpu.SemaphoreType.DMA((NZ, 2)),
            pltpu.SemaphoreType.DMA((NZ, 2)),
            pltpu.SemaphoreType.DMA((NZ,)),
            pltpu.SemaphoreType.DMA((NZ,)),
            pltpu.SemaphoreType.DMA((NZ, EXP - 1)),
            pltpu.SemaphoreType.DMA((NZ, EXP - 1)),
            pltpu.SemaphoreType.DMA((NZ - DOWN_HELD, 2)),
            pltpu.SemaphoreType.DMA((NZ - DOWN_HELD, 2)),
        ],
        compiler_params=pltpu.CompilerParams(collective_id=3, has_side_effects=True, vmem_limit_bytes=48 * MIB),
        cost_estimate=pl.CostEstimate(flops=2_500_000_000, bytes_accessed=32 * MIB, transcendentals=100_000),
        name="experts",
    )(arrived, in_hbm(weights), hidden, ids, gates)[0]


def body(queries, keys, values, w_out, residual, norm_gain, expert_ids, gate_weights, w_gate, w_up, w_down):
    attn, weights = attention(queries, keys, values, w_gate[0], w_up[0], w_down[0])
    arrived, hidden, weights = project(attn, w_out, residual, norm_gain.reshape(1, D), expert_ids, weights)
    return experts(arrived, weights, hidden, expert_ids, gate_weights)


def solution(mesh):
    placed = (
        P("ctx", "exp"),
        P("ctx", None),
        P("ctx", None),
        P("exp", None),
        P(("ctx", "exp"), None),
        P(),
        P(("ctx", "exp"), None),
        P(("ctx", "exp"), None),
        P("exp", "ctx", None),
        P("exp", "ctx", None),
        P("exp", None, "ctx"),
    )
    return jax.shard_map(
        body, mesh=mesh, in_specs=placed, out_specs=P(("ctx", "exp"), None), check_vma=False
    )
```

```python
import functools
import math

import jax
import jax.numpy as jnp
from jax import lax
from jax.experimental import pallas as pl
from jax.experimental.pallas import tpu as pltpu
from jax.sharding import PartitionSpec as P

D = 4096
HQ = 64
KVH = 4
HD = 128
FF = 768
EXPERTS = 8
CAP = 16
ROWS = 32
NX, NZ, NC = 2, 8, 2
CTX = NX * NZ * NC
EXP = 8
TOK = 256
HALF = 128
HEADS = HQ // EXP
MESH = pl.DeviceIdType.MESH
MIB = 1 << 20
F32 = jnp.float32
BF16 = jnp.bfloat16


def remote(src, dst, send, recv, ctx, exp):
    return pltpu.make_async_remote_copy(
        src_ref=src, dst_ref=dst, send_sem=send, recv_sem=recv, device_id=(ctx, exp), device_id_type=MESH
    )


def greet(peers):
    barrier = pltpu.get_barrier_semaphore()
    for ctx, exp in peers:
        pl.semaphore_signal(barrier, inc=1, device_id=(ctx, exp), device_id_type=MESH)
    pl.semaphore_wait(barrier, len(peers))


def place():
    me = lax.axis_index("ctx")
    return me, lax.axis_index("exp"), me // (NZ * NC), (me // NC) % NZ, me % NC


def chunk(x, z, core):
    return x * (NZ * NC) + lax.rem(z + 2 * NZ, NZ) * NC + core


def chip(x, z):
    return x * NZ + lax.rem(z + 2 * NZ, NZ)


def hop_copies(w_ref, kind, hop, snd, rcv, slot):
    me, ex, x, z, core = place()
    out = []
    for way, (xx, step) in enumerate(((x, 1), (1 - x, -1))):
        ref = w_ref.at[chip(xx, z - step * hop), :, kind]
        out.append(remote(ref, ref, snd.at[slot, way], rcv.at[slot, way], chunk(x, z + step, core), ex))
    return out


def start_hop(*a):
    for c in hop_copies(*a):
        c.start()


def finish_hop(w_ref, kind, hop, snd, rcv, slot):
    me, ex, x, z, core = place()
    for way, (xx, step) in enumerate(((x, 1), (1 - x, -1))):
        ref = w_ref.at[chip(xx, z - step * (hop + 1)), :, kind]
        remote(ref, ref, snd.at[slot, way], rcv.at[slot, way], me, ex).wait_recv()
    for c in hop_copies(w_ref, kind, hop, snd, rcv, slot):
        c.wait_send()


def ring_peers():
    me, ex, x, z, core = place()
    return [(chunk(x, z + 1, core), ex), (chunk(x, z - 1, core), ex)]


HBM = pltpu.HBM
TILES = FF // NC // 128
FH = FF // NC
CHIPS = CTX // NC
WSHAPE = HBM((CHIPS, NC, 3 * FH, 128), BF16)


def in_hbm(x):
    return pltpu.with_memory_space_constraint(x, HBM)


PRE, DOWN = pl.ds(0, 2 * FH), pl.ds(2 * FH, FH)
ATTN_HOPS, PROJ_HOPS = 2, 5
ATTN_DOWN, PROJ_DOWN = 1, 3
DOWN_HELD = ATTN_DOWN + PROJ_DOWN + 1


CK = NC * TOK
KB = 2 * CK
TR = 128
QROWS = HEADS * HALF
SCALE2 = math.log2(math.e) / math.sqrt(HD)
NP = 2 * TILES + 1
FAR = NZ // 2


def attn_kernel(
    q_ref, k_ref, v_ref, g_ref, u_ref, d_ref, o_ref, w_ref,
    kv, qs, acc, m_sc, vx,
    kv_l, q_l, own_s, own_r, ring_s, ring_r, sib_s, sib_r, w_l, w_s, w_r, wx_s, wx_r, snd, rcv, d_s, d_r,
):
    me, ex, x, z, core = place()
    up, down = chunk(x, z + 1, core), chunk(x, z - 1, core)
    across, sib = chunk(1 - x, z, core), chunk(x, z, 1 - core)
    here = chip(x, z)
    head = pl.ds(pl.multiple_of((ex // 2) * HD, HD), HD)

    def part(c, cc):
        return kv.at[c, :, pl.ds(pl.multiple_of(cc * TOK, TOK), TOK)]

    def pieces(half):
        for a, ref in enumerate((g_ref, u_ref)):
            for t in range(TILES):
                cols = pl.ds(pl.multiple_of(half * FH + t * 128, 128), 128)
                yield ref.at[:, cols], w_ref.at[here, core, pl.ds((a * TILES + t) * 128, 128)]
        yield d_ref.at[pl.ds(pl.multiple_of(half * FH, FH), FH)], w_ref.at[here, core, pl.ds(2 * FH, FH)]

    rows0 = pl.ds(pl.multiple_of(core * TOK, TOK), TOK)
    kvl = [
        pltpu.make_async_copy(ref.at[:, head], kv.at[here, i, rows0], kv_l.at[i]) for i, ref in enumerate((k_ref, v_ref))
    ]
    ql = [
        pltpu.make_async_copy(
            q_ref.at[pl.ds(a * HALF, HALF), pl.ds(h * HD, HD)], qs.at[a, pl.ds(h * HALF, HALF)], q_l.at[a, h]
        )
        for a in range(2)
        for h in range(HEADS)
    ]
    kept = [pltpu.make_async_copy(src, dst, w_l.at[i]) for i, (src, dst) in enumerate(pieces(core))]
    for c in kvl + ql + kept:
        c.start()
    greet([(up, ex), (down, ex), (across, ex), (sib, ex)])
    for c in kvl:
        c.wait()

    def piece(flow, step, cc):
        return part(chip(x if flow in (0, 2) else 1 - x, z - step if flow in (0, 3) else z + step), cc)

    def hop(flow, step):
        ref = piece(flow, step, core)
        target = up if flow in (0, 3) else down
        return remote(ref, ref, ring_s.at[flow, step], ring_r.at[flow, step], target, ex)

    def share(flow, step):
        ref = piece(flow, step, core)
        return remote(ref, ref, sib_s.at[flow, step], sib_r.at[flow, step], sib, ex)

    def shared(way, step):
        ref = piece(way, step, 1 - core)
        remote(ref, ref, sib_s.at[way, step], sib_r.at[way, step], me, ex).wait_recv()

    own = part(here, core)
    cross = remote(own, own, own_s, own_r, across, ex)
    cross.start()
    hop(0, 0).start()
    hop(2, 0).start()
    share(0, 0).start()
    other = part(chip(1 - x, z), core)
    remote(other, other, own_s, own_r, me, ex).wait_recv()
    hop(1, 0).start()
    hop(3, 0).start()
    share(1, 0).start()
    wsent = [remote(src, dst, w_s.at[i], w_r.at[i], sib, ex) for i, (src, dst) in enumerate(pieces(1 - core))]
    for c in wsent:
        c.start()
    wcross = remote(w_ref.at[here], w_ref.at[here], wx_s, wx_r, across, ex)
    vx[:, HD:] = jnp.ones((KB, HD), BF16)
    m_sc[...] = jnp.full_like(m_sc, -1e30)
    acc[...] = jnp.zeros_like(acc)
    for c in ql:
        c.wait()

    def block(which, start, c0, c1, masked):
        k = jnp.concatenate([kv[c0, 0], kv[c1, 0]], axis=0)
        for t in range(QROWS // TR):
            rows = pl.ds(t * TR, TR)
            s = lax.dot_general(qs[which, rows, :], k, (((1,), (1,)), ((), ())), preferred_element_type=F32)
            if masked:
                row = lax.broadcasted_iota(jnp.int32, (TR, KB), 0) % HALF + start
                lane = lax.broadcasted_iota(jnp.int32, (TR, KB), 1)
                col = lane + jnp.where(lane < CK, c0 * CK, c1 * CK - CK)
                s = jnp.where(col <= row, s, -1e30)
            old = m_sc[which, rows, :]
            new = jnp.maximum(old, jnp.max(s, axis=1, keepdims=True))
            p = jnp.exp2((s - new[:, :1]) * SCALE2)
            factor = jnp.exp2((old - new) * SCALE2)
            m_sc[which, rows, :] = new
            acc[which, rows, :] = acc[which, rows, :] * jnp.concatenate([factor, factor], axis=1) + jnp.dot(
                p.astype(BF16), vx[...], preferred_element_type=F32
            )

    @pl.loop(0, NZ)
    def _(u):
        step = jnp.where(u == NZ - 3, FAR, u)

        @pl.when(((u >= 1) & (u < FAR)) | (u == NZ - 3))
        def _():
            for flow in (0, 2, 1, 3):
                far = FAR - flow // 2

                @pl.when(step <= far)
                def _():
                    ref = piece(flow, step, core)
                    remote(ref, ref, ring_s.at[flow, step - 1], ring_r.at[flow, step - 1], me, ex).wait_recv()

                    @pl.when(step < far)
                    def _():
                        hop(flow, step).start()

                    share(flow, step).start()

        @pl.when(u == 1)
        def _():
            for i in range(NP):
                kept[i].wait()
                wsent[i].wait_recv()
            wcross.start()

        @pl.when(u == FAR)
        def _():
            wcross.wait_recv()
            start_hop(w_ref, PRE, 0, snd, rcv, 0)
            start_hop(w_ref, DOWN, 0, d_s, d_r, 0)

        @pl.when(u == NZ - 1)
        def _():
            finish_hop(w_ref, PRE, 0, snd, rcv, 0)
            start_hop(w_ref, PRE, 1, snd, rcv, 1)

        away = (u + 1) // 2
        odd = u % 2 == 1
        c0 = chip(jnp.where(odd | (u == 0), x, 1 - x), z - away)
        c1 = chip(jnp.where(odd & (u != NZ - 1), x, 1 - x), z + away)
        ends = (u == 0) | (u == NZ - 1)
        for flows, when in (((0, 1), ends), ((0, 2), odd & jnp.logical_not(ends)), ((1, 3), jnp.logical_not(odd | ends))):

            @pl.when(when)
            def _():
                for flow in flows:
                    shared(flow, away)

        vx[pl.ds(0, CK), :HD] = kv[c0, 1]
        vx[pl.ds(CK, CK), :HD] = kv[c1, 1]

        @pl.loop(0, 2)
        def _(which):
            start = me * TOK + which * HALF
            full = jnp.maximum(c0, c1) * CK + CK - 1 <= start
            some = jnp.minimum(c0, c1) * CK <= start

            @pl.when(full)
            def _():
                block(which, start, c0, c1, False)

            @pl.when(some & jnp.logical_not(full))
            def _():
                block(which, start, c0, c1, True)

    for which in range(2):
        for h in range(HEADS):
            rows = pl.ds(h * HALF, HALF)
            made = (acc[which, rows, :HD] / acc[which, rows, HD:]).astype(BF16)
            o_ref[pl.ds(which * HALF, HALF), pl.ds(h * HD, HD)] = made
    finish_hop(w_ref, PRE, 1, snd, rcv, 1)
    finish_hop(w_ref, DOWN, 0, d_s, d_r, 0)
    cross.wait_send()
    wcross.wait_send()
    for c in wsent:
        c.wait_send()
    for flow in range(4):
        for step in range(0 if flow < 2 else 1, FAR - flow // 2 + 1):
            share(flow, step).wait_send()
        for step in range(FAR - flow // 2):
            hop(flow, step).wait_send()


def attention(queries, keys, values, w_gate, w_up, w_down):
    dma = pltpu.SemaphoreType.DMA
    hbm = pl.BlockSpec(memory_space=HBM)
    return pl.pallas_call(
        attn_kernel,
        out_shape=(jax.ShapeDtypeStruct((TOK, HEADS * HD), BF16), WSHAPE),
        in_specs=[hbm] * 6,
        out_specs=(pl.BlockSpec(memory_space=pltpu.VMEM), hbm),
        scratch_shapes=[
            pltpu.VMEM((CHIPS, 2, CK, HD), BF16),
            pltpu.VMEM((2, QROWS, HD), BF16),
            pltpu.VMEM((2, QROWS, 2 * HD), F32),
            pltpu.VMEM((2, QROWS, HD), F32),
            pltpu.VMEM((KB, 2 * HD), BF16),
            dma((2,)), dma((2, HEADS)),
            dma, dma,
            dma((4, FAR)), dma((4, FAR)), dma((4, FAR + 1)), dma((4, FAR + 1)),
            dma((NP,)), dma((NP,)), dma((NP,)), dma, dma,
            dma((ATTN_HOPS, 2)), dma((ATTN_HOPS, 2)), dma((ATTN_DOWN, 2)), dma((ATTN_DOWN, 2)),
        ],
        compiler_params=pltpu.CompilerParams(collective_id=1, has_side_effects=True, vmem_limit_bytes=32 * MIB),
        cost_estimate=pl.CostEstimate(flops=9_000_000_000, bytes_accessed=64 * MIB, transcendentals=9_000_000),
        name="attention",
    )(*(in_hbm(a) for a in (queries, keys, values, w_gate, w_up, w_down)))


def slots(ids_ref):
    lane = lax.broadcasted_iota(jnp.int32, (ROWS, EXPERTS * CAP), 1)
    named = [ids_ref[:, k : k + 1] == lane // CAP for k in range(2)]
    has = (named[0] | named[1]).astype(F32)
    tri = lax.broadcasted_iota(jnp.int32, (ROWS, ROWS), 1) < lax.broadcasted_iota(jnp.int32, (ROWS, ROWS), 0)
    place = jnp.dot(tri.astype(F32).astype(BF16), has.astype(BF16), preferred_element_type=F32)
    here = place == (lane % CAP).astype(F32)
    return [(n & here).astype(F32) for n in named]


NB = 512
PG = 2
PC = D // PG
WL = D // NB


def project_kernel(
    o_ref, w_hbm, res_ref, gain_ref, ids_ref, e_in, arr_ref, hid_ref, e_ref,
    w, part, recv, norm, out, w_sem, rs_s, rs_r, a_s, a_r, f_s, f_r, snd, rcv, d_s, d_r,
):
    me, ex, x, z, core = place()
    sib = me + 1 - 2 * core

    def load(n):
        cols = pl.ds(pl.multiple_of(n * NB, NB), NB)
        return pltpu.make_async_copy(w_hbm.at[:, cols], w.at[n], w_sem.at[n])

    for n in range(WL):
        load(n).start()
    peers = [lax.rem(ex + d, EXP) for d in range(1, EXP)]
    greet(ring_peers() + [(sib, ex)] + [(me, p) for p in peers])
    start_hop(e_ref, PRE, ATTN_HOPS, snd, rcv, 0)
    start_hop(e_ref, DOWN, ATTN_DOWN, d_s, d_r, 0)

    def next_down(i):
        finish_hop(e_ref, DOWN, ATTN_DOWN + i, d_s, d_r, i)
        if i + 1 < PROJ_DOWN:
            start_hop(e_ref, DOWN, ATTN_DOWN + i + 1, d_s, d_r, i + 1)

    def next_hop(i):
        finish_hop(e_ref, PRE, ATTN_HOPS + i, snd, rcv, i)
        if i + 1 < PROJ_HOPS:
            start_hop(e_ref, PRE, ATTN_HOPS + i + 1, snd, rcv, i + 1)

    def share(g, d):
        p = lax.rem(ex + d, EXP)
        return remote(part.at[g, p], recv.at[g, d - 1], rs_s.at[g, d - 1], rs_r.at[g, d - 1], me, p)

    for g in range(PG):

        @pl.loop(0, PC // NB)
        def _(i):
            n = g * (PC // NB) + i
            load(n).wait()
            got = jnp.dot(o_ref[...], w[n], preferred_element_type=F32).astype(BF16)
            cols = pl.ds(pl.multiple_of(i * NB, NB), NB)
            for b in range(EXP):
                part[g, b, :, cols] = got[b * ROWS : (b + 1) * ROWS, :]

        for d in range(1, EXP):
            share(g, d).start()

    next_hop(0)
    next_down(0)
    for g in range(PG):
        if g == 0:
            next_hop(1)
        for d in range(1, EXP):
            share(g, d).wait_recv()

        @pl.loop(0, PC // NB)
        def _(i):
            cols = pl.ds(pl.multiple_of(i * NB, NB), NB)
            total = part[g, ex, :, cols].astype(F32)
            for d in range(EXP - 1):
                total += recv[g, d, :, cols].astype(F32)
            full = pl.ds(pl.multiple_of(g * PC + i * NB, NB), NB)
            hid_ref[:, full] = (res_ref[:, full].astype(F32) + total).astype(BF16)

    state = hid_ref[...].astype(F32)
    inv = 1.0 / jnp.sqrt(jnp.mean(state * state, axis=1, keepdims=True) + 1e-06)
    norm[...] = (state * inv * gain_ref[...].astype(F32)).astype(BF16)
    first, second = slots(ids_ref)
    table = (first + second).T.astype(BF16)
    out[...] = jnp.dot(table, norm[...], preferred_element_type=F32).astype(BF16).reshape(EXPERTS, CAP, D)

    def give_rows(d):
        p = lax.rem(ex + d, EXP)
        return remote(out.at[p], arr_ref.at[0, ex], a_s.at[d - 1], a_r.at[d - 1], me, p)

    def forward(d):
        source = lax.rem(ex + EXP - d, EXP)
        return remote(arr_ref.at[0, source], arr_ref.at[1, source], f_s.at[d], f_r.at[d], sib, ex)

    for d in range(1, EXP):
        give_rows(d).start()
    arr_ref[0, ex] = out[ex]
    forward(0).start()
    next_hop(2)
    next_down(1)
    for d in range(1, EXP):
        if d == EXP // 2:
            next_hop(3)
        source = lax.rem(ex + EXP - d, EXP)
        remote(out.at[ex], arr_ref.at[0, source], a_s.at[d - 1], a_r.at[d - 1], me, ex).wait_recv()
        forward(d).start()
    for d in range(EXP):
        forward(d).wait()
    next_hop(4)
    next_down(2)
    for d in range(1, EXP):
        for g in range(PG):
            share(g, d).wait_send()
        give_rows(d).wait_send()


def project(attn, w_out, residual, gain, ids, weights):
    dma = pltpu.SemaphoreType.DMA
    vmem, hbm = pl.BlockSpec(memory_space=pltpu.VMEM), pl.BlockSpec(memory_space=HBM)
    return pl.pallas_call(
        project_kernel,
        out_shape=(
            jax.ShapeDtypeStruct((NC, EXPERTS, CAP, D), BF16),
            jax.ShapeDtypeStruct((ROWS, D), BF16),
            WSHAPE,
        ),
        in_specs=[vmem, hbm, vmem, vmem, vmem, hbm],
        out_specs=(vmem, vmem, hbm),
        input_output_aliases={5: 2},
        scratch_shapes=[
            pltpu.VMEM((WL, HEADS * HD, NB), BF16),
            pltpu.VMEM((PG, EXP, ROWS, PC), BF16),
            pltpu.VMEM((PG, EXP - 1, ROWS, PC), BF16),
            pltpu.VMEM((ROWS, D), BF16),
            pltpu.VMEM((EXPERTS, CAP, D), BF16),
            dma((WL,)), dma((PG, EXP - 1)), dma((PG, EXP - 1)), dma((EXP - 1,)), dma((EXP - 1,)),
            dma((EXP,)), dma((EXP,)), dma((PROJ_HOPS, 2)), dma((PROJ_HOPS, 2)),
            dma((PROJ_DOWN, 2)), dma((PROJ_DOWN, 2)),
        ],
        compiler_params=pltpu.CompilerParams(collective_id=2, has_side_effects=True, vmem_limit_bytes=40 * MIB),
        cost_estimate=pl.CostEstimate(flops=2_200_000_000, bytes_accessed=64 * MIB, transcendentals=0),
        name="project_dispatch",
    )(attn, in_hbm(w_out), residual, gain, ids, in_hbm(weights))


SLOTS = EXPERTS * CAP
DEPTH = NC * 128
GCOLS = NC * DEPTH


def expert_kernel(
    arr_ref, w_in, hid_ref, ids_ref, gates_ref, o_ref, w_hbm,
    w, pre, act, mine, theirs, other, res, got, p_sem, d_sem, x_s, x_r, r_s, r_r, d_s, d_r,
):
    me, ex, x, z, core = place()
    sib = me + 1 - 2 * core

    def at(step, way):
        return chip(x, z - step) if way == 0 else chip(1 - x, z + step)

    def load(kind, sem, step, way):
        c = at(step, way)
        return pltpu.make_async_copy(w_hbm.at[c, :, kind], w.at[c, :, kind], sem.at[step, way])

    for step in range(NZ):
        for way in range(2):
            load(PRE, p_sem, step, way).start()
    for step in range(DOWN_HELD):
        for way in range(2):
            load(DOWN, d_sem, step, way).start()
    peers = [lax.rem(ex + d, EXP) for d in range(1, EXP)]
    greet(ring_peers() + [(sib, ex)] + [(me, p) for p in peers])
    start_hop(w_hbm, DOWN, DOWN_HELD - 1, d_s, d_r, 0)
    pre[...] = jnp.zeros_like(pre)

    def use(step):
        for way in range(2):
            load(PRE, p_sem, step, way).wait()
            j = at(step, way)
            cols = pl.ds(pl.multiple_of(j * DEPTH, DEPTH), DEPTH)
            rows = arr_ref[:, :, :, cols].reshape(NC * SLOTS, DEPTH)
            tiles = [
                jnp.concatenate([w[j, c, pl.ds(t * 128, 128)] for c in range(NC)], axis=0) for t in range(2 * TILES)
            ]
            pre[...] += jnp.dot(rows, jnp.concatenate(tiles, axis=1), preferred_element_type=F32)

    def next_down(i):
        slot = i - DOWN_HELD + 1
        finish_hop(w_hbm, DOWN, i, d_s, d_r, slot)
        if i + 1 < NZ - 1:
            start_hop(w_hbm, DOWN, i + 1, d_s, d_r, slot + 1)
        for way in range(2):
            load(DOWN, d_sem, i + 1, way).start()

    for half in range(2):

        @pl.loop(half * NZ // 2, (half + 1) * NZ // 2)
        def _(step):
            use(step)

        next_down(DOWN_HELD - 1 + half)

    gate = pre[:, :FH]
    act[...] = (gate / (1.0 + jnp.exp(-gate)) * pre[:, FH:]).astype(BF16)

    def swap(t):
        return remote(theirs.at[t], other.at[t], x_s.at[t], x_r.at[t], sib, ex)

    def give(t, d):
        p = lax.rem(ex + d, EXP)
        return remote(res.at[t, p], got.at[t, ex], r_s.at[t, d - 1], r_r.at[t, d - 1], me, p)

    def finish(t):
        swap(t).wait_recv()
        res[t] = (mine[t] + other[t]).astype(BF16).reshape(EXPERTS, CAP, GCOLS)
        for d in range(1, EXP):
            give(t, d).start()
        got[t, ex] = res[t, ex]

    first, second = slots(ids_ref)
    picks = jnp.concatenate([first, second], axis=0).astype(BF16)
    weight = [gates_ref[:, k : k + 1] for k in range(2)]

    def combine(t):
        for d in range(1, EXP):
            source = lax.rem(ex + EXP - d, EXP)
            remote(res.at[t, ex], got.at[t, source], r_s.at[t, d - 1], r_r.at[t, d - 1], me, ex).wait_recv()
        both = jnp.dot(picks, got[t].reshape(SLOTS, GCOLS), preferred_element_type=F32)
        total = weight[0] * both[:ROWS] + weight[1] * both[ROWS:]
        for way in range(2):
            cols = pl.ds(pl.multiple_of(at(t, way) * DEPTH, DEPTH), DEPTH)
            part = total[:, way * DEPTH : (way + 1) * DEPTH]
            o_ref[:, cols] = (hid_ref[:, cols].astype(F32) + part).astype(BF16)

    for t in range(NZ):
        if t in TAKEN:
            next_down(DOWN_HELD + 1 + TAKEN.index(t))
        for way in range(2):
            load(DOWN, d_sem, t, way).wait()
            down = jnp.concatenate([w[at(t, way), c, DOWN] for c in range(NC)], axis=1)
            made = jnp.dot(act[...], down, preferred_element_type=F32)
            mine[t, :, way * DEPTH : (way + 1) * DEPTH] = made[:SLOTS]
            theirs[t, :, way * DEPTH : (way + 1) * DEPTH] = made[SLOTS:]
        swap(t).start()
        if t >= 1:
            finish(t - 1)
        if t >= LAG:
            combine(t - LAG)
    finish(NZ - 1)
    for t in range(NZ - LAG, NZ):
        combine(t)
    for t in range(NZ):
        swap(t).wait_send()
        for d in range(1, EXP):
            give(t, d).wait_send()


LAG = 4
TAKEN = (2,)


def experts(arrived, weights, hidden, ids, gates):
    vmem, hbm = pl.BlockSpec(memory_space=pltpu.VMEM), pl.BlockSpec(memory_space=HBM)
    return pl.pallas_call(
        expert_kernel,
        out_shape=(jax.ShapeDtypeStruct((ROWS, D), BF16), WSHAPE),
        in_specs=[vmem, hbm, vmem, vmem, vmem],
        out_specs=(vmem, hbm),
        input_output_aliases={1: 1},
        scratch_shapes=[
            pltpu.VMEM((CHIPS, NC, 3 * FH, 128), BF16),
            pltpu.VMEM((NC * SLOTS, 2 * FH), F32),
            pltpu.VMEM((NC * SLOTS, FH), BF16),
            pltpu.VMEM((NZ, SLOTS, GCOLS), F32),
            pltpu.VMEM((NZ, SLOTS, GCOLS), F32),
            pltpu.VMEM((NZ, SLOTS, GCOLS), F32),
            pltpu.VMEM((NZ, EXPERTS, CAP, GCOLS), BF16),
            pltpu.VMEM((NZ, EXPERTS, CAP, GCOLS), BF16),
            pltpu.SemaphoreType.DMA((NZ, 2)),
            pltpu.SemaphoreType.DMA((NZ, 2)),
            pltpu.SemaphoreType.DMA((NZ,)),
            pltpu.SemaphoreType.DMA((NZ,)),
            pltpu.SemaphoreType.DMA((NZ, EXP - 1)),
            pltpu.SemaphoreType.DMA((NZ, EXP - 1)),
            pltpu.SemaphoreType.DMA((NZ - DOWN_HELD, 2)),
            pltpu.SemaphoreType.DMA((NZ - DOWN_HELD, 2)),
        ],
        compiler_params=pltpu.CompilerParams(collective_id=3, has_side_effects=True, vmem_limit_bytes=48 * MIB),
        cost_estimate=pl.CostEstimate(flops=2_500_000_000, bytes_accessed=32 * MIB, transcendentals=100_000),
        name="experts",
    )(arrived, in_hbm(weights), hidden, ids, gates)[0]


def body(queries, keys, values, w_out, residual, norm_gain, expert_ids, gate_weights, w_gate, w_up, w_down):
    attn, weights = attention(queries, keys, values, w_gate[0], w_up[0], w_down[0])
    arrived, hidden, weights = project(attn, w_out, residual, norm_gain.reshape(1, D), expert_ids, weights)
    return experts(arrived, weights, hidden, expert_ids, gate_weights)


def solution(mesh):
    placed = (
        P("ctx", "exp"),
        P("ctx", None),
        P("ctx", None),
        P("exp", None),
        P(("ctx", "exp"), None),
        P(),
        P(("ctx", "exp"), None),
        P(("ctx", "exp"), None),
        P("exp", "ctx", None),
        P("exp", "ctx", None),
        P("exp", None, "ctx"),
    )
    return jax.shard_map(
        body, mesh=mesh, in_specs=placed, out_specs=P(("ctx", "exp"), None), check_vma=False
    )
```
